512 devices in a mesh: win: 8 (over y, core), frame: 64 (over z, x).
Axes of the slice: x: 4, y: 4, z: 16, core: 2. Of those that a mesh axis runs over, the one named last changes fastest.
Arguments:
- distances: float32 [32, 131072], P(None, 'frame'), may hold values from 0.05 to 9
- sample_ids: int32 [131072], P('frame'), may hold values from 0 to 4095, as said below
- lengths: int32 [64], replicated, may hold values from 1 to 2048, 81920 in all
- stiffness: float32 [4096, 32], P('win'), may hold values from 0.5 to 19
- centers: float32 [4096, 32], P('win'), may hold values from 0.1 to 3.7
Outputs:
- free_energy: float32 [4096], P('win')
The draws below stay inside these ranges and needn't reach their ends.
Inputs may be any that keep to these rules, and one draw needn't show every extreme that they name: The frames of a block occupy its first slots; the lengths add up to 81920 and the largest is 2048. `sample_ids`: slots beyond a block's length hold ids that are not used; exactly 512 windows appear in no slot.
All inputs are finite; a program needn't handle non-finite values.
Results may differ from the reference program's by a relative error of at most 0.0003.
Values sent between devices are 32-bit elements; how exact they have to be, the bound alone decides.
No kernel may reach another device: no remote copies, remote signals or barrier semaphores. Data moves between devices by JAX's collectives and lax.ppermute only.
A program may use at most 64 MiB of HBM per device.

```python
import math
import jax
import jax.numpy as jnp
import numpy as np
from jax import lax

NA = 32
FR_DEV = 2048
ITERS = 2
K = 4096
NBLK = 64
FRAMES = 131072
TOTAL = 81920


def unused_count():
    return max(K // 8, 2)


def window_order(key):
    return jax.random.permutation(jax.random.fold_in(key, 101), K).astype(jnp.int32)


def draw_sample_ids(key, part):
    order_table = window_order(key)
    chosen = jax.random.randint(jax.random.fold_in(key, 102), (FRAMES,), unused_count(), K, dtype=jnp.int32)
    return jnp.take(order_table, chosen).astype(jnp.int32)


def stiffness_table(key):
    restraint_scale = jnp.exp(jax.random.uniform(jax.random.fold_in(key, 121), (NA,), jnp.float32, 0.0, math.log(10.0)))
    spread = 0.25 * jnp.clip(jax.random.normal(jax.random.fold_in(key, 122), (K, NA), jnp.float32), -2.5, 2.5)
    return restraint_scale[None, :] * jnp.exp(spread)


def centre_table(key):
    speeds = jax.random.uniform(jax.random.fold_in(key, 131), (NA,), jnp.float32, 1.0 / 450.0, 1.0 / 250.0)
    phases = jax.random.uniform(jax.random.fold_in(key, 132), (NA,), jnp.float32, 0.0, 2.0 * math.pi)
    positions = jnp.arange(K, dtype=jnp.float32)
    centre_path = 3.0 + 0.5 * jnp.sin(2.0 * math.pi * positions[:, None] * speeds[None, :] + phases[None, :])
    wobble = 0.06 * jnp.clip(jax.random.normal(jax.random.fold_in(key, 133), (K, NA), jnp.float32), -2.5, 2.5)
    return centre_path + wobble


def draw_centers(key, part):
    return centre_table(key)


def draw_stiffness(key, part):
    return stiffness_table(key)


def draw_distances(key, part):
    frame_ids = draw_sample_ids(key, part)
    own_centres = jnp.take(centre_table(key), frame_ids, axis=0)
    own_stiffness = jnp.take(stiffness_table(key), frame_ids, axis=0)
    jitter = jnp.clip(jax.random.normal(jax.random.fold_in(key, 141), (FRAMES, NA), jnp.float32), -2.5, 2.5)
    values = own_centres + jitter / jnp.sqrt(own_stiffness)
    return jnp.clip(values, 0.05, 9.0).T


def profile(count, total, reach, slope):
    loads = [(1 << 20) // math.isqrt(standing ** slope) + 1 for standing in range(2, count + 1)]
    surplus, given = total - reach - (count - 1), [1] * (count - 1)
    while surplus > 0:
        candidates = [i for i in range(count - 1) if given[i] < reach]
        mass, left = sum([loads[i] for i in candidates]), surplus
        for i in candidates:
            extra = min(reach - given[i], max(1, left * loads[i] // mass), surplus)
            given[i] = given[i] + extra
            surplus = surplus - extra
    return np.array([reach] + given)


def ragged_sizes(key, count, total, bound, slope):
    if count == 2:
        one = jax.random.randint(key, (), max(1, total - bound), min(bound, total - 1) + 1)
        return jnp.stack([one, total - one])
    sizes = jnp.asarray(profile(count, total, bound, slope), jnp.int32)
    pairs = (count - 1) // 2
    source_of, sink = sizes[1:1 + 2 * pairs:2], sizes[2:2 + 2 * pairs:2]
    margin = jnp.minimum(source_of - 1, bound - sink)
    moved = jax.random.randint(jax.random.fold_in(key, 1), (pairs,), 0, 1 << 20) % (margin + 1)
    sizes = sizes.at[1:1 + 2 * pairs:2].set(source_of - moved).at[2:2 + 2 * pairs:2].set(sink + moved)
    return sizes[jax.random.permutation(jax.random.fold_in(key, 2), count)]


def setup_inputs(seed: int = 0) -> dict:
    splits = jax.random.split(jax.random.key(seed), 6)
    distances = draw_distances(jax.random.fold_in(splits[5], 71), 0)
    sample_ids = draw_sample_ids(jax.random.fold_in(splits[5], 71), 0)
    lengths = ragged_sizes(splits[2], NBLK, TOTAL, FR_DEV, 2).astype(jnp.int32)
    stiffness = draw_stiffness(jax.random.fold_in(splits[5], 71), 0)
    centers = draw_centers(jax.random.fold_in(splits[5], 71), 0)
    return dict(distances=distances, sample_ids=sample_ids, lengths=lengths, stiffness=stiffness, centers=centers)


floor_value = -1.0e30


def coefficients(stiffness, centers):
    constant = jnp.sum(0.5 * stiffness * centers * centers, axis=1, keepdims=True)
    return jnp.concatenate([constant, -stiffness * centers, 0.5 * stiffness], axis=1)


def features(separations):
    unit_row = jnp.ones((1, separations.shape[1]), separations.dtype)
    return jnp.concatenate([unit_row, separations, separations * separations], axis=0)


def energies(coef_rows, separations):
    return jnp.dot(coef_rows, features(separations), precision=lax.Precision.HIGHEST, preferred_element_type=jnp.float32)


def reference(distances, sample_ids, lengths, stiffness, centers):
    coef_rows = coefficients(stiffness, centers)
    window_total = stiffness.shape[0]
    block_total = lengths.shape[0]
    capacity = distances.shape[1] // block_total
    slot_index = jnp.arange(capacity, dtype=jnp.int32)
    usable = slot_index[None, :] < lengths[:, None]
    counts = jax.ops.segment_sum(usable.reshape(-1).astype(jnp.float32), sample_ids, num_segments=window_total)
    sampled = counts > 0.5
    log_count = jnp.log(jnp.maximum(counts, 1.0))
    restraints = distances.shape[0]
    frame_blocks = distances.reshape(restraints, block_total, capacity).transpose(1, 0, 2)
    free_energy = jnp.zeros((window_total,), jnp.float32)
    for iteration in range(ITERS):
        shifted = log_count + free_energy

        def den_block(separations):
            energy = energies(coef_rows, separations)
            exponent = jnp.where(sampled[:, None], shifted[:, None] - energy, floor_value)
            highest = jnp.max(exponent, axis=0)
            summed = jnp.sum(jnp.where(sampled[:, None], jnp.exp(exponent - highest[None, :]), 0.0), axis=0)
            return highest + jnp.log(summed)

        log_den = lax.map(den_block, frame_blocks)

        def frame_block(running, inputs):
            separations, den_block_values, use_block = inputs
            energy = energies(coef_rows, separations)
            exponent = jnp.where(use_block[None, :], -energy - den_block_values[None, :], floor_value)
            highest = jnp.max(exponent, axis=1)
            summed = jnp.sum(jnp.where(use_block[None, :], jnp.exp(exponent - highest[:, None]), 0.0), axis=1)
            top_all = jnp.maximum(running[0], highest)
            merged = running[1] * jnp.exp(running[0] - top_all) + summed * jnp.exp(highest - top_all)
            return (top_all, merged), None

        start_value = (jnp.full((window_total,), floor_value, jnp.float32), jnp.zeros((window_total,), jnp.float32))
        running, _ = lax.scan(frame_block, start_value, (frame_blocks, log_den, usable))
        free_energy = -(running[0] + jnp.log(running[1]))
    return free_energy
```

```python
import jax
import jax.numpy as jnp
from jax import lax
from jax.sharding import PartitionSpec as P

ITERS = 2


floor_value = -1e30


def coefficients(stiffness, centers):
    constant = jnp.sum(0.5 * stiffness * centers * centers, axis=1, keepdims=True)
    return jnp.concatenate([constant, -stiffness * centers, 0.5 * stiffness], axis=1)


def features(separations):
    unit_row = jnp.ones((1, separations.shape[1]), separations.dtype)
    return jnp.concatenate([unit_row, separations, separations * separations], axis=0)


def energies(coef_rows, separations):
    return jnp.dot(
        coef_rows,
        features(separations),
        precision=lax.Precision.HIGHEST,
        preferred_element_type=jnp.float32,
    )


def share(values, axis):
    copies = jnp.broadcast_to(values[None, :], (lax.axis_size(axis), values.shape[0]))
    return lax.all_to_all(copies, axis, split_axis=0, concat_axis=0, tiled=True)


def log_sum_exp(values, axis):
    highest = jnp.max(values, axis=axis, keepdims=True)
    return jnp.squeeze(highest, axis) + jnp.log(jnp.sum(jnp.exp(values - highest), axis=axis))


def on_device(distances, sample_ids, lengths, stiffness, centers):
    local_windows = stiffness.shape[0]
    capacity = distances.shape[1]
    own_length = lax.dynamic_index_in_dim(lengths, lax.axis_index("frame"), keepdims=False)
    slot_usable = jnp.arange(capacity, dtype=jnp.int32) < own_length
    numbers = lax.axis_index("win") * local_windows + jnp.arange(local_windows, dtype=jnp.int32)
    ids = jnp.where(slot_usable, sample_ids, -1)
    local_counts = jnp.sum((ids[None, :] == numbers[:, None]).astype(jnp.float32), axis=1)
    counts = jnp.sum(share(local_counts, "frame"), axis=0)
    energy = energies(coefficients(stiffness, centers), distances)
    sampled = counts > 0.5
    log_count = jnp.log(jnp.maximum(counts, 1.0))
    free_energy = jnp.zeros((local_windows,), jnp.float32)
    for iteration in range(ITERS):
        shifted = jnp.where(sampled, log_count + free_energy, floor_value)
        own_den = log_sum_exp(shifted[:, None] - energy, 0)
        log_den = log_sum_exp(share(own_den, "win"), 0)
        log_den = jnp.where(slot_usable, log_den, -floor_value)
        own_total = log_sum_exp(-energy - log_den[None, :], 1)
        free_energy = -log_sum_exp(share(own_total, "frame"), 0)
    return free_energy


def solution(mesh):
    return jax.shard_map(
        on_device,
        mesh=mesh,
        in_specs=(P(None, "frame"), P("frame"), P(), P("win", None), P("win", None)),
        out_specs=P("win"),
        check_vma=False,
    )
```

```python
import functools

import jax
import jax.numpy as jnp
from jax import lax
from jax.experimental import pallas as pl
from jax.experimental.pallas import tpu as pltpu
from jax.sharding import PartitionSpec as P

ITERS = 2
LANES = 128
ROWS = 64

floor_value = -1e30

in_vmem = pl.BlockSpec(memory_space=pltpu.VMEM)
in_smem = pl.BlockSpec(memory_space=pltpu.SMEM)
small_grant = pltpu.CompilerParams(vmem_limit_bytes=12 << 20)


def log_sum_exp(values):
    highest = jnp.max(values, axis=0)
    return highest + jnp.log(jnp.sum(jnp.exp(values - highest[None]), axis=0))


def count_kernel(lengths_ref, ids_ref, out_ref):
    groups = out_ref.shape[1]
    capacity = ids_ref.shape[1]
    own_length = lengths_ref[lax.axis_index("frame")]
    local = ids_ref[...] - lax.axis_index("win") * (groups * LANES)
    slots = lax.broadcasted_iota(jnp.int32, (1, capacity), 1)
    local = jnp.where(slots < own_length, local, -1)
    group = jnp.where(local < 0, -1, lax.shift_right_logical(local, 7))
    place = jnp.bitwise_and(local, LANES - 1)
    in_group = lax.broadcasted_iota(jnp.int32, (8, capacity), 0) == group
    in_place = lax.broadcasted_iota(jnp.int32, (LANES, capacity), 0) == place
    counts = lax.dot_general(
        in_group.astype(jnp.float32).astype(jnp.bfloat16),
        in_place.astype(jnp.float32).astype(jnp.bfloat16),
        (((1,), (1,)), ((), ())),
        preferred_element_type=jnp.float32,
    )
    out_ref[...] = jnp.broadcast_to(counts[None, :groups], out_ref.shape)


def energy_kernel(stiffness_ref, centers_ref, distances_ref, energy_ref):
    stiffness, centers = stiffness_ref[...], centers_ref[...]
    constant = jnp.sum(0.5 * stiffness * centers * centers, axis=0, keepdims=True)
    first = lax.broadcasted_iota(jnp.int32, (8, constant.shape[1]), 0) == 0
    constant_rows = jnp.where(first, jnp.broadcast_to(constant, first.shape), 0.0)
    coef_rows = jnp.concatenate([-stiffness * centers, 0.5 * stiffness, constant_rows], axis=0).T
    step = 512
    unit_rows = jnp.where(lax.broadcasted_iota(jnp.int32, (8, step), 0) == 0, 1.0, 0.0)

    def one(block, carry):
        columns = pl.ds(pl.multiple_of(block * step, step), step)
        separations = distances_ref[:, columns]
        features = jnp.concatenate([separations, separations * separations, unit_rows], axis=0)
        energy_ref[:, columns] = jnp.dot(
            coef_rows, features, precision=lax.Precision.HIGHEST, preferred_element_type=jnp.float32
        )
        return carry

    lax.fori_loop(0, distances_ref.shape[1] // step, one, 0)


def denominators(shifted, energy_ref, out_ref, column_ref, row_ref):
    groups = shifted.shape[0]
    for group in range(groups):
        spread = jnp.broadcast_to(shifted[group : group + 1], (LANES, LANES))
        column_ref[group * LANES : (group + 1) * LANES, :] = spread.T
    windows = column_ref.shape[0]
    chunks = [slice(start, start + ROWS) for start in range(0, windows, ROWS)]

    def one(block, carry):
        columns = pl.ds(pl.multiple_of(block * LANES, LANES), LANES)
        tops = [
            jnp.max((column_ref[rows, :] - energy_ref[rows, columns]).reshape(-1, 8, LANES), axis=0)
            for rows in chunks
        ]
        highest = jnp.max(functools.reduce(jnp.maximum, tops), axis=0, keepdims=True)
        sums = [
            jnp.sum(
                jnp.exp(column_ref[rows, :] - energy_ref[rows, columns] - highest).reshape(-1, 8, LANES),
                axis=0,
            )
            for rows in chunks
        ]
        total = jnp.sum(functools.reduce(jnp.add, sums), axis=0, keepdims=True)
        row_ref[pl.ds(block, 1), :] = highest + jnp.log(total)
        return carry

    lax.fori_loop(0, energy_ref.shape[1] // LANES, one, 0, unroll=2)
    out_ref[...] = jnp.broadcast_to(row_ref[...][None], out_ref.shape)


def first_kernel(shared_ref, energy_ref, counts_ref, out_ref, column_ref, row_ref):
    counts = jnp.sum(shared_ref[...], axis=0)
    counts_ref[...] = counts
    shifted = jnp.where(counts > 0.5, jnp.log(jnp.maximum(counts, 1.0)), floor_value)
    denominators(shifted, energy_ref, out_ref, column_ref, row_ref)


def next_kernel(shared_ref, counts_ref, energy_ref, out_ref, column_ref, row_ref):
    counts = counts_ref[...]
    free_energy = -log_sum_exp(shared_ref[...])
    shifted = jnp.where(counts > 0.5, jnp.log(jnp.maximum(counts, 1.0)) + free_energy, floor_value)
    denominators(shifted, energy_ref, out_ref, column_ref, row_ref)


def window_kernel(lengths_ref, shared_ref, energy_ref, out_ref, den_ref, top_ref, sum_ref):
    own_length = lengths_ref[lax.axis_index("frame")]
    blocks, windows = shared_ref.shape[1], energy_ref.shape[0]
    log_den = log_sum_exp(shared_ref[...])
    slots = (
        lax.broadcasted_iota(jnp.int32, (blocks, LANES), 0) * LANES
        + lax.broadcasted_iota(jnp.int32, (blocks, LANES), 1)
    )
    den_ref[...] = jnp.where(slots < own_length, log_den, -floor_value)

    def one(chunk, carry):
        rows = pl.ds(pl.multiple_of(chunk * ROWS, ROWS), ROWS)
        top = jnp.full((ROWS, LANES), 2.0 * floor_value, jnp.float32)
        for block in range(blocks):
            columns = slice(block * LANES, (block + 1) * LANES)
            top = jnp.maximum(top, -energy_ref[rows, columns] - den_ref[block : block + 1, :])
        total = jnp.zeros((ROWS, LANES), jnp.float32)
        for block in range(blocks):
            columns = slice(block * LANES, (block + 1) * LANES)
            total = total + jnp.exp(-energy_ref[rows, columns] - den_ref[block : block + 1, :] - top)
        top_ref[rows, :] = top
        sum_ref[rows, :] = total
        return carry

    lax.fori_loop(0, windows // ROWS, one, 0)
    for group in range(windows // LANES):
        rows = slice(group * LANES, (group + 1) * LANES)
        tops, sums = top_ref[rows, :].T, sum_ref[rows, :].T
        highest = jnp.max(tops, axis=0, keepdims=True)
        total = jnp.sum(sums * jnp.exp(tops - highest), axis=0, keepdims=True)
        row = highest + jnp.log(total)
        out_ref[:, group : group + 1, :] = jnp.broadcast_to(row[None], (out_ref.shape[0], 1, LANES))


def exchange(copies, axis):
    return lax.all_to_all(copies, axis, split_axis=0, concat_axis=0, tiled=True)


def on_device(distances, sample_ids, lengths, stiffness, centers):
    windows, capacity = stiffness.shape[0], distances.shape[1]
    groups, blocks = windows // LANES, capacity // LANES
    frame_devices, win_devices = lax.axis_size("frame"), lax.axis_size("win")
    f32 = jnp.float32
    to_frame = jax.ShapeDtypeStruct((frame_devices, groups, LANES), f32)
    to_win = jax.ShapeDtypeStruct((win_devices, blocks, LANES), f32)
    energy_cost = pl.CostEstimate(
        flops=12 * 2 * distances.shape[0] * windows * capacity, bytes_accessed=4 * windows * capacity, transcendentals=0
    )
    local_counts = pl.pallas_call(
        count_kernel, out_shape=to_frame, in_specs=[in_smem, in_vmem], out_specs=in_vmem, compiler_params=small_grant, name="count_windows"
    )(lengths, sample_ids.reshape(1, capacity))
    shared = exchange(local_counts, "frame")
    energy = pl.pallas_call(
        energy_kernel,
        out_shape=jax.ShapeDtypeStruct((windows, capacity), f32),
        in_specs=[in_vmem] * 3,
        out_specs=in_vmem,
        cost_estimate=energy_cost,
        compiler_params=small_grant,
        name="energies",
    )(stiffness.T, centers.T, distances)
    scratch = [pltpu.VMEM((windows, LANES), f32), pltpu.VMEM((blocks, LANES), f32)]
    counts, own_den = pl.pallas_call(
        first_kernel,
        out_shape=(jax.ShapeDtypeStruct((groups, LANES), f32), to_win),
        in_specs=[in_vmem] * 2,
        out_specs=(in_vmem, in_vmem),
        scratch_shapes=scratch,
        compiler_params=small_grant,
        name="first_denominators",
    )(shared, energy)
    for iteration in range(ITERS):
        own_total = pl.pallas_call(
            window_kernel,
            out_shape=to_frame,
            in_specs=[in_smem, in_vmem, in_vmem],
            out_specs=in_vmem,
            scratch_shapes=[pltpu.VMEM((blocks, LANES), f32)] + [pltpu.VMEM((windows, LANES), f32)] * 2,
            compiler_params=small_grant,
            name="window_totals",
        )(lengths, exchange(own_den, "win"), energy)
        shared = exchange(own_total, "frame")
        if iteration < ITERS - 1:
            own_den = pl.pallas_call(
                next_kernel,
                out_shape=to_win,
                in_specs=[in_vmem] * 3,
                out_specs=in_vmem,
                scratch_shapes=scratch,
                compiler_params=small_grant,
                name="next_denominators",
            )(shared, counts, energy)
    return -log_sum_exp(shared).reshape(windows)


def solution(mesh):
    return jax.shard_map(
        on_device,
        mesh=mesh,
        in_specs=(P(None, "frame"), P("frame"), P(), P("win", None), P("win", None)),
        out_specs=P("win"),
        check_vma=False,
    )
```

```python
import functools
import math

import jax
import jax.numpy as jnp
from jax import lax
from jax.experimental import pallas as pl
from jax.experimental.pallas import tpu as pltpu
from jax.sharding import PartitionSpec as P


ITERS = 2
LANES = 128
ROWS = 64
STEP = 512

floor_value = -1e30
log2_e = 1.0 / math.log(2.0)
least_sum = 2.0**-80
most_sum = 2.0**100

in_vmem = pl.BlockSpec(memory_space=pltpu.VMEM)
in_hbm = pl.BlockSpec(memory_space=pltpu.HBM)
grant = pltpu.CompilerParams(vmem_limit_bytes=12 << 20)
wide_grant = pltpu.CompilerParams(vmem_limit_bytes=52 * 10**6)


def log2(values):
    return jnp.log(values) * log2_e


def log2_sum(values):
    highest = jnp.max(values, axis=0)
    return highest + log2(jnp.sum(jnp.exp2(values - highest[None]), axis=0))


def together(pairs, sems):
    copies = [pltpu.make_async_copy(*pair, sems.at[place]) for place, pair in enumerate(pairs)]
    for copy in copies:
        copy.start()
    for copy in copies:
        copy.wait()


def count_kernel(lengths_hbm, ids_hbm, out_hbm, lengths_ref, ids_ref, out_ref, in_sems, out_sem):
    together([(lengths_hbm, lengths_ref), (ids_hbm, ids_ref)], in_sems)
    groups = out_ref.shape[1]
    capacity = ids_ref.shape[1]
    own_length = lengths_ref[lax.axis_index("frame")]
    local = ids_ref[...] - lax.axis_index("win") * (groups * LANES)
    slots = lax.broadcasted_iota(jnp.int32, (1, capacity), 1)
    local = jnp.where(slots < own_length, local, -1)
    group = jnp.where(local < 0, -1, lax.shift_right_logical(local, 7))
    place = jnp.bitwise_and(local, LANES - 1)
    in_group = lax.broadcasted_iota(jnp.int32, (8, capacity), 0) == group
    in_place = lax.broadcasted_iota(jnp.int32, (LANES, capacity), 0) == place
    counts = lax.dot_general(
        in_group.astype(jnp.float32).astype(jnp.bfloat16),
        in_place.astype(jnp.float32).astype(jnp.bfloat16),
        (((1,), (1,)), ((), ())),
        preferred_element_type=jnp.float32,
    )
    out_ref[...] = jnp.broadcast_to(counts[None, :groups], out_ref.shape)
    copy = pltpu.make_async_copy(out_ref, out_hbm, out_sem)
    copy.start()
    copy.wait()


def energy_kernel(
    lengths_hbm, stiffness_hbm, centers_hbm, distances_hbm, fall_hbm, tops_hbm,
    lengths_ref, stiffness_ref, centers_ref, distances_ref, fall_ref, tops_ref, in_sems, fall_sems, tops_sem,
):
    together(
        [
            (lengths_hbm, lengths_ref),
            (stiffness_hbm, stiffness_ref),
            (centers_hbm, centers_ref),
            (distances_hbm, distances_ref),
        ],
        in_sems,
    )
    own_length = lengths_ref[lax.axis_index("frame")]
    stiffness, centers = stiffness_ref[...] * log2_e, centers_ref[...]
    constant = jnp.sum(-0.5 * stiffness * centers * centers, axis=0, keepdims=True)
    first = lax.broadcasted_iota(jnp.int32, (8, constant.shape[1]), 0) == 0
    constant_rows = jnp.where(first, jnp.broadcast_to(constant, first.shape), 0.0)
    coef_rows = jnp.concatenate([stiffness * centers, -0.5 * stiffness, constant_rows], axis=0).T
    unit_rows = jnp.where(lax.broadcasted_iota(jnp.int32, (8, STEP), 0) == 0, 1.0, 0.0)
    steps = distances_ref.shape[1] // STEP

    def columns(step):
        return pl.ds(pl.multiple_of(step * STEP, STEP), STEP)

    def send(step):
        return pltpu.make_async_copy(
            fall_ref.at[:, columns(step)], fall_hbm.at[:, columns(step)], fall_sems.at[step]
        )

    def one(step, carry):
        separations = distances_ref[:, columns(step)]
        features = jnp.concatenate([separations, separations * separations, unit_rows], axis=0)
        exponents = jnp.dot(
            coef_rows, features, precision=lax.Precision.HIGHEST, preferred_element_type=jnp.float32
        )
        top = jnp.max(exponents, axis=0, keepdims=True)
        fall_ref[:, columns(step)] = exponents - top
        send(step).start()
        for part in range(STEP // LANES):
            tops_ref[0, pl.ds(step * (STEP // LANES) + part, 1), :] = top[:, part * LANES : (part + 1) * LANES]
        return carry

    lax.fori_loop(0, steps, one, 0)
    blocks = tops_ref.shape[1]
    slots = (
        lax.broadcasted_iota(jnp.int32, (blocks, LANES), 0) * LANES
        + lax.broadcasted_iota(jnp.int32, (blocks, LANES), 1)
    )
    tops_ref[1] = jnp.where(slots < own_length, tops_ref[0], floor_value)
    copy = pltpu.make_async_copy(tops_ref, tops_hbm, tops_sem)
    copy.start()
    copy.wait()
    for step in range(steps):
        send(step).wait()


def denominators(shifted, arrive, fall_ref, tops_ref, out_ref, column_ref, part_ref, row_ref):
    groups = shifted.shape[0]
    most = jnp.max(jnp.max(shifted, axis=0, keepdims=True), axis=1, keepdims=True)
    for group in range(groups):
        spread = jnp.broadcast_to(shifted[group : group + 1] - most, (LANES, LANES))
        column_ref[group * LANES : (group + 1) * LANES, :] = spread.T
    windows, capacity = fall_ref.shape
    blocks = capacity // LANES
    chunks = [slice(start, start + ROWS) for start in range(0, windows, ROWS)]

    def columns(block):
        return pl.ds(pl.multiple_of(block * LANES, LANES), LANES)

    def one(block, carry):
        sums = [
            jnp.sum(
                jnp.exp2(fall_ref[rows, columns(block)] + column_ref[rows, :]).reshape(-1, 8, LANES), axis=0
            )
            for rows in chunks
        ]
        part_ref[block] = functools.reduce(jnp.add, sums)
        return carry

    steps = capacity // STEP
    for step in range(steps):
        arrive(step)
        lax.fori_loop(step * (STEP // LANES), (step + 1) * (STEP // LANES), one, 0, unroll=True)
    totals = jnp.sum(part_ref[...], axis=1)
    row_ref[...] = tops_ref[...] + most + log2(totals)

    @pl.when(jnp.min(totals) < least_sum)
    def _():
        def exact(block, carry):
            tops = [
                jnp.max((fall_ref[rows, columns(block)] + column_ref[rows, :]).reshape(-1, 8, LANES), axis=0)
                for rows in chunks
            ]
            highest = jnp.max(functools.reduce(jnp.maximum, tops), axis=0, keepdims=True)
            sums = [
                jnp.sum(
                    jnp.exp2(fall_ref[rows, columns(block)] + column_ref[rows, :] - highest).reshape(-1, 8, LANES),
                    axis=0,
                )
                for rows in chunks
            ]
            total = jnp.sum(functools.reduce(jnp.add, sums), axis=0, keepdims=True)
            row_ref[pl.ds(block, 1), :] = tops_ref[pl.ds(block, 1), :] + most + highest + log2(total)
            return carry

        lax.fori_loop(0, blocks, exact, 0)

    out_ref[...] = jnp.broadcast_to(row_ref[...][None], out_ref.shape)


def first_kernel(
    shared_ref, fall_hbm, tops_hbm, counts_ref, out_ref, fall_ref, tops_ref, column_ref, part_ref, row_ref, sems, tops_sem
):
    def fetch(step):
        columns = slice(step * STEP, (step + 1) * STEP)
        return pltpu.make_async_copy(fall_hbm.at[:, columns], fall_ref.at[:, columns], sems.at[step])

    tops_copy = pltpu.make_async_copy(tops_hbm, tops_ref, tops_sem)
    for step in range(fall_hbm.shape[1] // STEP):
        fetch(step).start()
    tops_copy.start()
    counts = jnp.sum(shared_ref[...], axis=0)
    counts_ref[...] = counts
    shifted = jnp.where(counts > 0.5, log2(jnp.maximum(counts, 1.0)), floor_value)
    tops_copy.wait()
    denominators(
        shifted, lambda step: fetch(step).wait(), fall_ref, tops_ref.at[0], out_ref, column_ref, part_ref, row_ref
    )


def next_kernel(shared_ref, counts_ref, fall_ref, tops_ref, out_ref, column_ref, part_ref, row_ref):
    counts = counts_ref[...]
    free_energy = -log2_sum(shared_ref[...])
    shifted = jnp.where(counts > 0.5, log2(jnp.maximum(counts, 1.0)) + free_energy, floor_value)
    denominators(
        shifted, lambda step: None, fall_ref, tops_ref.at[0], out_ref, column_ref, part_ref, row_ref
    )


def window_kernel(shared_ref, fall_ref, tops_ref, out_ref, den_ref, top_ref, sum_ref, row_ref):
    blocks, windows = shared_ref.shape[1], fall_ref.shape[0]
    groups = windows // LANES
    den_ref[...] = log2_sum(shared_ref[...]) - tops_ref[1]

    def rows_of(chunk):
        return pl.ds(pl.multiple_of(chunk * ROWS, ROWS), ROWS)

    def exponents(rows, block):
        return fall_ref[rows, block * LANES : (block + 1) * LANES] - den_ref[block : block + 1, :]

    def one(chunk, carry):
        rows = rows_of(chunk)
        total = jnp.exp2(exponents(rows, 0))
        for block in range(1, blocks):
            total = total + jnp.exp2(exponents(rows, block))
        sum_ref[rows, :] = total
        return carry

    lax.fori_loop(0, windows // ROWS, one, 0)
    least, most = [], []
    for group in range(groups):
        total = jnp.sum(sum_ref[group * LANES : (group + 1) * LANES, :].T, axis=0, keepdims=True)
        row_ref[group : group + 1, :] = log2(total)
        least.append(total)
        most.append(total)
    lowest = jnp.min(functools.reduce(jnp.minimum, least))
    highest = jnp.max(functools.reduce(jnp.maximum, most))

    @pl.when(jnp.logical_not(jnp.logical_and(lowest > least_sum, highest < most_sum)))
    def _():
        def exact(chunk, carry):
            rows = rows_of(chunk)
            top = exponents(rows, 0)
            for block in range(1, blocks):
                top = jnp.maximum(top, exponents(rows, block))
            total = jnp.exp2(exponents(rows, 0) - top)
            for block in range(1, blocks):
                total = total + jnp.exp2(exponents(rows, block) - top)
            top_ref[rows, :] = top
            sum_ref[rows, :] = total
            return carry

        lax.fori_loop(0, windows // ROWS, exact, 0)
        for group in range(groups):
            rows = slice(group * LANES, (group + 1) * LANES)
            tops, sums = top_ref[rows, :].T, sum_ref[rows, :].T
            top = jnp.max(tops, axis=0, keepdims=True)
            total = jnp.sum(sums * jnp.exp2(tops - top), axis=0, keepdims=True)
            row_ref[group : group + 1, :] = top + log2(total)

    out_ref[...] = jnp.broadcast_to(row_ref[...][None], out_ref.shape)


def exchange(copies, axis):
    return lax.all_to_all(copies, axis, split_axis=0, concat_axis=0, tiled=True)


def on_device(distances, sample_ids, lengths, stiffness, centers):
    windows, capacity = stiffness.shape[0], distances.shape[1]
    groups, blocks, steps = windows // LANES, capacity // LANES, capacity // STEP
    f32, dma = jnp.float32, pltpu.SemaphoreType.DMA
    to_frame = jax.ShapeDtypeStruct((lax.axis_size("frame"), groups, LANES), f32)
    to_win = jax.ShapeDtypeStruct((lax.axis_size("win"), blocks, LANES), f32)
    lengths_here = pltpu.SMEM(lengths.shape, jnp.int32)
    local_counts = pl.pallas_call(
        count_kernel,
        out_shape=to_frame,
        in_specs=[in_hbm] * 2,
        out_specs=in_hbm,
        scratch_shapes=[
            lengths_here,
            pltpu.VMEM((1, capacity), jnp.int32),
            pltpu.VMEM(to_frame.shape, f32),
            dma((2,)),
            dma,
        ],
        name="count_windows",
    )(lengths, sample_ids.reshape(1, capacity))
    shared = exchange(local_counts, "frame")
    energy_shapes = (
        jax.ShapeDtypeStruct((windows, capacity), f32),
        jax.ShapeDtypeStruct((2, blocks, LANES), f32),
    )
    fall, tops = pl.pallas_call(
        energy_kernel,
        out_shape=energy_shapes,
        in_specs=[in_hbm] * 4,
        out_specs=(in_hbm, in_hbm),
        scratch_shapes=[
            lengths_here,
            pltpu.VMEM((stiffness.shape[1], windows), f32),
            pltpu.VMEM((stiffness.shape[1], windows), f32),
            pltpu.VMEM(distances.shape, f32),
            pltpu.VMEM((windows, capacity), f32),
            pltpu.VMEM((2, blocks, LANES), f32),
            dma((4,)),
            dma((steps,)),
            dma,
        ],
        cost_estimate=pl.CostEstimate(
            flops=24 * distances.shape[0] * windows * capacity,
            bytes_accessed=4 * windows * capacity,
            transcendentals=0,
        ),
        name="energies",
    )(lengths, stiffness.T, centers.T, distances)
    den_scratch = [
        pltpu.VMEM((windows, LANES), f32),
        pltpu.VMEM((blocks, 8, LANES), f32),
        pltpu.VMEM((blocks, LANES), f32),
    ]
    counts, own_den, fall, tops = pl.pallas_call(
        first_kernel,
        out_shape=(jax.ShapeDtypeStruct((groups, LANES), f32), to_win, *energy_shapes),
        in_specs=[in_vmem, in_hbm, in_hbm],
        out_specs=(in_vmem,) * 4,
        scratch_shapes=[
            *den_scratch,
            dma((steps,)),
            dma,
        ],
        compiler_params=wide_grant,
        name="first_denominators",
    )(shared, fall, tops)
    for iteration in range(ITERS):
        own_total = pl.pallas_call(
            window_kernel,
            out_shape=to_frame,
            in_specs=[in_vmem] * 3,
            out_specs=in_vmem,
            scratch_shapes=[
                pltpu.VMEM((blocks, LANES), f32),
                pltpu.VMEM((windows, LANES), f32),
                pltpu.VMEM((windows, LANES), f32),
                pltpu.VMEM((groups, LANES), f32),
            ],
            compiler_params=grant,
            name="window_totals",
        )(exchange(own_den, "win"), fall, tops)
        shared = exchange(own_total, "frame")
        if iteration < ITERS - 1:
            own_den = pl.pallas_call(
                next_kernel,
                out_shape=to_win,
                in_specs=[in_vmem] * 4,
                out_specs=in_vmem,
                scratch_shapes=den_scratch,
                compiler_params=grant,
                name="next_denominators",
            )(shared, counts, fall, tops)
    return (-math.log(2.0) * log2_sum(shared)).reshape(windows)


def solution(mesh):
    return jax.shard_map(
        on_device,
        mesh=mesh,
        in_specs=(P(None, "frame"), P("frame"), P(), P("win", None), P("win", None)),
        out_specs=P("win"),
        check_vma=False,
    )
```

```python
import functools
import math

import jax
import jax.numpy as jnp
from jax import lax
from jax.experimental import pallas as pl
from jax.experimental.pallas import tpu as pltpu
from jax.sharding import PartitionSpec as P


ITERS = 2
LANES = 128
ROWS = 64
STEP = 512

floor_value = -1e30
log2_e = 1.0 / math.log(2.0)
FAR = 1
least_sum = 2.0**-80
most_sum = 2.0**100

in_vmem = pl.BlockSpec(memory_space=pltpu.VMEM)
in_hbm = pl.BlockSpec(memory_space=pltpu.HBM)
grant = pltpu.CompilerParams(vmem_limit_bytes=12 << 20)


def log2(values):
    return jnp.log(values) * log2_e


def log2_sum(values):
    highest = jnp.max(values, axis=0)
    return highest + log2(jnp.sum(jnp.exp2(values - highest[None]), axis=0))


def together(pairs, sems):
    copies = [pltpu.make_async_copy(*pair, sems.at[place]) for place, pair in enumerate(pairs)]
    for copy in copies:
        copy.start()
    for copy in copies:
        copy.wait()


def count_kernel(lengths_hbm, ids_hbm, out_hbm, lengths_ref, ids_ref, out_ref, in_sems, out_sem):
    together([(lengths_hbm, lengths_ref), (ids_hbm, ids_ref)], in_sems)
    groups = out_ref.shape[1]
    capacity = ids_ref.shape[1]
    own_length = lengths_ref[lax.axis_index("frame")]
    local = ids_ref[...] - lax.axis_index("win") * (groups * LANES)
    slots = lax.broadcasted_iota(jnp.int32, (1, capacity), 1)
    local = jnp.where(slots < own_length, local, -1)
    group = jnp.where(local < 0, -1, lax.shift_right_logical(local, 7))
    place = jnp.bitwise_and(local, LANES - 1)
    in_group = lax.broadcasted_iota(jnp.int32, (8, capacity), 0) == group
    in_place = lax.broadcasted_iota(jnp.int32, (LANES, capacity), 0) == place
    counts = lax.dot_general(
        in_group.astype(jnp.float32).astype(jnp.bfloat16),
        in_place.astype(jnp.float32).astype(jnp.bfloat16),
        (((1,), (1,)), ((), ())),
        preferred_element_type=jnp.float32,
    )
    out_ref[...] = jnp.broadcast_to(counts[None, :groups], out_ref.shape)
    copy = pltpu.make_async_copy(out_ref, out_hbm, out_sem)
    copy.start()
    copy.wait()


def energy_kernel(
    stiffness_hbm, centers_hbm, distances_hbm, near_ref, tops_ref, far_hbm,
    stiffness_ref, centers_ref, distances_ref, far_ref, in_sems, far_sem,
):
    together(
        [
            (stiffness_hbm, stiffness_ref),
            (centers_hbm, centers_ref),
            (distances_hbm, distances_ref),
        ],
        in_sems,
    )
    stiffness, centers = stiffness_ref[...] * log2_e, centers_ref[...]
    constant = jnp.sum(-0.5 * stiffness * centers * centers, axis=0, keepdims=True)
    first = lax.broadcasted_iota(jnp.int32, (8, constant.shape[1]), 0) == 0
    constant_rows = jnp.where(first, jnp.broadcast_to(constant, first.shape), 0.0)
    coef_rows = jnp.concatenate([stiffness * centers, -0.5 * stiffness, constant_rows], axis=0).T
    unit_rows = jnp.where(lax.broadcasted_iota(jnp.int32, (8, STEP), 0) == 0, 1.0, 0.0)

    def one(step, to_ref, to):
        start = pl.multiple_of(step * STEP, STEP)
        separations = distances_ref[:, pl.ds(start, STEP)]
        features = jnp.concatenate([separations, separations * separations, unit_rows], axis=0)
        exponents = jnp.dot(
            coef_rows, features, precision=lax.Precision.HIGHEST, preferred_element_type=jnp.float32
        )
        top = jnp.max(exponents, axis=0, keepdims=True)
        to_ref[:, pl.ds(to, STEP)] = exponents - top
        for part in range(STEP // LANES):
            tops_ref[pl.ds(step * (STEP // LANES) + part, 1), :] = top[:, part * LANES : (part + 1) * LANES]

    near_steps = near_ref.shape[1] // STEP
    copy = pltpu.make_async_copy(far_ref, far_hbm, far_sem)
    one(near_steps, far_ref, 0)
    copy.start()

    def near(step, carry):
        one(step, near_ref, pl.multiple_of(step * STEP, STEP))
        return carry

    lax.fori_loop(0, near_steps, near, 0)
    copy.wait()


def denominators(shifted, arrive, parts, tops_ref, out_ref, column_ref, part_ref, row_ref):
    groups = shifted.shape[0]
    most = jnp.max(jnp.max(shifted, axis=0, keepdims=True), axis=1, keepdims=True)
    for group in range(groups):
        spread = jnp.broadcast_to(shifted[group : group + 1] - most, (LANES, LANES))
        column_ref[group * LANES : (group + 1) * LANES, :] = spread.T
    windows = column_ref.shape[0]
    chunks = [slice(start, start + ROWS) for start in range(0, windows, ROWS)]

    def exponents(ref, rows, block):
        return (ref[rows, pl.ds(pl.multiple_of(block * LANES, LANES), LANES)] + column_ref[rows, :]).reshape(
            -1, 8, LANES
        )

    done = 0
    for part, ref in enumerate(parts):
        if part:
            arrive()
        count = ref.shape[1] // LANES

        def one(block, carry, ref=ref, done=done):
            sums = [jnp.sum(jnp.exp2(exponents(ref, rows, block)), axis=0) for rows in chunks]
            part_ref[done + block] = functools.reduce(jnp.add, sums)
            return carry

        lax.fori_loop(0, count, one, 0, unroll=4)
        done += count
    totals = jnp.sum(part_ref[...], axis=1)
    out_ref[...] = jnp.broadcast_to((tops_ref[...] + most + log2(totals))[None], out_ref.shape)

    @pl.when(jnp.min(totals) < least_sum)
    def _():
        done = 0
        for ref in parts:
            count = ref.shape[1] // LANES

            def exact(block, carry, ref=ref, done=done):
                tops = [jnp.max(exponents(ref, rows, block), axis=0) for rows in chunks]
                highest = jnp.max(functools.reduce(jnp.maximum, tops), axis=0, keepdims=True)
                sums = [jnp.sum(jnp.exp2(exponents(ref, rows, block) - highest), axis=0) for rows in chunks]
                total = jnp.sum(functools.reduce(jnp.add, sums), axis=0, keepdims=True)
                row_ref[pl.ds(done + block, 1), :] = highest + log2(total)
                return carry

            lax.fori_loop(0, count, exact, 0)
            done += count
        out_ref[...] = jnp.broadcast_to((tops_ref[...] + most + row_ref[...])[None], out_ref.shape)


def first_kernel(
    lengths_hbm, shared_ref, near_ref, tops_ref, far_hbm, counts_ref, out_ref, far_ref, used_ref,
    column_ref, part_ref, row_ref, lengths_ref, sem, lengths_sem,
):
    copy = pltpu.make_async_copy(far_hbm, far_ref, sem)
    lengths_copy = pltpu.make_async_copy(lengths_hbm, lengths_ref, lengths_sem)
    copy.start()
    lengths_copy.start()
    counts = jnp.sum(shared_ref[...], axis=0)
    counts_ref[...] = counts
    shifted = jnp.where(counts > 0.5, log2(jnp.maximum(counts, 1.0)), floor_value)
    denominators(shifted, copy.wait, (near_ref, far_ref), tops_ref, out_ref, column_ref, part_ref, row_ref)
    lengths_copy.wait()
    own_length = lengths_ref[lax.axis_index("frame")]
    slots = (
        lax.broadcasted_iota(jnp.int32, tops_ref.shape, 0) * LANES
        + lax.broadcasted_iota(jnp.int32, tops_ref.shape, 1)
    )
    used_ref[...] = jnp.where(slots < own_length, tops_ref[...], floor_value)


def next_kernel(shared_ref, counts_ref, near_ref, tops_ref, far_ref, out_ref, column_ref, part_ref, row_ref):
    counts = counts_ref[...]
    free_energy = -log2_sum(shared_ref[...])
    shifted = jnp.where(counts > 0.5, log2(jnp.maximum(counts, 1.0)) + free_energy, floor_value)
    denominators(shifted, lambda: None, (near_ref, far_ref), tops_ref, out_ref, column_ref, part_ref, row_ref)


def window_kernel(shared_ref, near_ref, used_ref, far_ref, out_ref, den_ref, top_ref, sum_ref, row_ref):
    windows, near_blocks, far_blocks = near_ref.shape[0], near_ref.shape[1] // LANES, far_ref.shape[1] // LANES
    groups = windows // LANES
    den_ref[...] = log2_sum(shared_ref[...]) - used_ref[...]

    def exponents(chunk):
        rows = pl.ds(pl.multiple_of(chunk * ROWS, ROWS), ROWS)
        for ref, done in ((near_ref, 0), (far_ref, near_blocks)):
            for block in range(ref.shape[1] // LANES):
                yield ref[rows, block * LANES : (block + 1) * LANES] - den_ref[done + block : done + block + 1, :]

    def one(chunk, carry):
        rows = pl.ds(pl.multiple_of(chunk * ROWS, ROWS), ROWS)
        sum_ref[rows, :] = functools.reduce(jnp.add, (jnp.exp2(each) for each in exponents(chunk)))
        return carry

    lax.fori_loop(0, windows // ROWS, one, 0)
    totals = []
    for group in range(groups):
        total = jnp.sum(sum_ref[group * LANES : (group + 1) * LANES, :].T, axis=0, keepdims=True)
        totals.append(total)
        row_ref[group : group + 1, :] = log2(total)
    out_ref[...] = jnp.broadcast_to(row_ref[...][None], out_ref.shape)
    lowest = jnp.min(functools.reduce(jnp.minimum, totals))
    highest = jnp.max(functools.reduce(jnp.maximum, totals))

    @pl.when(jnp.logical_not(jnp.logical_and(lowest > least_sum, highest < most_sum)))
    def _():
        def exact(chunk, carry):
            rows = pl.ds(pl.multiple_of(chunk * ROWS, ROWS), ROWS)
            top = functools.reduce(jnp.maximum, exponents(chunk))
            top_ref[rows, :] = top
            sum_ref[rows, :] = functools.reduce(jnp.add, (jnp.exp2(each - top) for each in exponents(chunk)))
            return carry

        lax.fori_loop(0, windows // ROWS, exact, 0)
        for group in range(groups):
            rows = slice(group * LANES, (group + 1) * LANES)
            tops, sums = top_ref[rows, :].T, sum_ref[rows, :].T
            top = jnp.max(tops, axis=0, keepdims=True)
            total = jnp.sum(sums * jnp.exp2(tops - top), axis=0, keepdims=True)
            row_ref[group : group + 1, :] = top + log2(total)
        out_ref[...] = jnp.broadcast_to(row_ref[...][None], out_ref.shape)


def exchange(copies, axis):
    return lax.all_to_all(copies, axis, split_axis=0, concat_axis=0, tiled=True)


def on_device(distances, sample_ids, lengths, stiffness, centers):
    windows, capacity = stiffness.shape[0], distances.shape[1]
    groups, blocks, steps = windows // LANES, capacity // LANES, capacity // STEP
    f32, dma = jnp.float32, pltpu.SemaphoreType.DMA
    to_frame = jax.ShapeDtypeStruct((lax.axis_size("frame"), groups, LANES), f32)
    to_win = jax.ShapeDtypeStruct((lax.axis_size("win"), blocks, LANES), f32)
    lengths_here = pltpu.SMEM(lengths.shape, jnp.int32)
    local_counts = pl.pallas_call(
        count_kernel,
        out_shape=to_frame,
        in_specs=[in_hbm] * 2,
        out_specs=in_hbm,
        scratch_shapes=[
            lengths_here,
            pltpu.VMEM((1, capacity), jnp.int32),
            pltpu.VMEM(to_frame.shape, f32),
            dma((2,)),
            dma,
        ],
        name="count_windows",
    )(lengths, sample_ids.reshape(1, capacity))
    shared = exchange(local_counts, "frame")
    far_frames = FAR * STEP
    near_shape = jax.ShapeDtypeStruct((windows, capacity - far_frames), f32)
    far_shape = jax.ShapeDtypeStruct((windows, far_frames), f32)
    tops_shape = jax.ShapeDtypeStruct((blocks, LANES), f32)
    near, tops, far = pl.pallas_call(
        energy_kernel,
        out_shape=(near_shape, tops_shape, far_shape),
        in_specs=[in_hbm] * 3,
        out_specs=(in_vmem, in_vmem, in_hbm),
        scratch_shapes=[
            pltpu.VMEM((stiffness.shape[1], windows), f32),
            pltpu.VMEM((stiffness.shape[1], windows), f32),
            pltpu.VMEM(distances.shape, f32),
            pltpu.VMEM(far_shape.shape, f32),
            dma((3,)),
            dma,
        ],
        compiler_params=grant,
        cost_estimate=pl.CostEstimate(
            flops=24 * distances.shape[0] * windows * capacity,
            bytes_accessed=4 * windows * capacity,
            transcendentals=0,
        ),
        name="energies",
    )(stiffness.T, centers.T, distances)
    den_scratch = [
        pltpu.VMEM((windows, LANES), f32),
        pltpu.VMEM((blocks, 8, LANES), f32),
        pltpu.VMEM((blocks, LANES), f32),
    ]
    counts, own_den, far, used = pl.pallas_call(
        first_kernel,
        out_shape=(jax.ShapeDtypeStruct((groups, LANES), f32), to_win, far_shape, tops_shape),
        in_specs=[in_hbm, in_vmem, in_vmem, in_vmem, in_hbm],
        out_specs=(in_vmem,) * 4,
        scratch_shapes=[*den_scratch, lengths_here, dma, dma],
        compiler_params=grant,
        name="first_denominators",
    )(lengths, shared, near, tops, far)
    for iteration in range(ITERS):
        own_total = pl.pallas_call(
            window_kernel,
            out_shape=to_frame,
            in_specs=[in_vmem] * 4,
            out_specs=in_vmem,
            scratch_shapes=[
                pltpu.VMEM((blocks, LANES), f32),
                pltpu.VMEM((windows, LANES), f32),
                pltpu.VMEM((windows, LANES), f32),
                pltpu.VMEM((groups, LANES), f32),
            ],
            compiler_params=grant,
            name="window_totals",
        )(exchange(own_den, "win"), near, used, far)
        shared = exchange(own_total, "frame")
        if iteration < ITERS - 1:
            own_den = pl.pallas_call(
                next_kernel,
                out_shape=to_win,
                in_specs=[in_vmem] * 5,
                out_specs=in_vmem,
                scratch_shapes=den_scratch,
                compiler_params=grant,
                name="next_denominators",
            )(shared, counts, near, tops, far)
    return (-math.log(2.0) * log2_sum(shared)).reshape(windows)


def solution(mesh):
    return jax.shard_map(
        on_device,
        mesh=mesh,
        in_specs=(P(None, "frame"), P("frame"), P(), P("win", None), P("win", None)),
        out_specs=P("win"),
        check_vma=False,
    )
```

```python
import functools
import math

import jax
import jax.numpy as jnp
from jax import lax
from jax.experimental import pallas as pl
from jax.experimental.pallas import tpu as pltpu
from jax.sharding import PartitionSpec as P


ITERS = 2
LANES = 128
ROWS = 64
STEP = 512

floor_value = -1e30
log2_e = 1.0 / math.log(2.0)
FAR = 1
least_sum = 2.0**-80
most_sum = 2.0**100

in_vmem = pl.BlockSpec(memory_space=pltpu.VMEM)
in_hbm = pl.BlockSpec(memory_space=pltpu.HBM)
grant = pltpu.CompilerParams(vmem_limit_bytes=12 << 20)


def hbm(array):
    return pltpu.with_memory_space_constraint(array, pltpu.HBM)


def log2(values):
    return jnp.log(values) * log2_e


def log2_sum(values):
    highest = jnp.max(values, axis=0)
    return highest + log2(jnp.sum(jnp.exp2(values - highest[None]), axis=0))


def together(pairs, sems):
    copies = [pltpu.make_async_copy(*pair, sems.at[place]) for place, pair in enumerate(pairs)]
    for copy in copies:
        copy.start()
    for copy in copies:
        copy.wait()


def count_kernel(lengths_hbm, ids_hbm, out_hbm, lengths_ref, ids_ref, out_ref, in_sems, out_sem):
    together([(lengths_hbm, lengths_ref), (ids_hbm, ids_ref)], in_sems)
    groups = out_ref.shape[1]
    capacity = ids_ref.shape[1]
    own_length = lengths_ref[lax.axis_index("frame")]
    local = ids_ref[...] - lax.axis_index("win") * (groups * LANES)
    slots = lax.broadcasted_iota(jnp.int32, (1, capacity), 1)
    local = jnp.where(slots < own_length, local, -1)
    group = jnp.where(local < 0, -1, lax.shift_right_logical(local, 7))
    place = jnp.bitwise_and(local, LANES - 1)
    in_group = lax.broadcasted_iota(jnp.int32, (8, capacity), 0) == group
    in_place = lax.broadcasted_iota(jnp.int32, (LANES, capacity), 0) == place
    counts = lax.dot_general(
        in_group.astype(jnp.float32).astype(jnp.bfloat16),
        in_place.astype(jnp.float32).astype(jnp.bfloat16),
        (((1,), (1,)), ((), ())),
        preferred_element_type=jnp.float32,
    )
    out_ref[...] = jnp.broadcast_to(counts[None, :groups], out_ref.shape)
    copy = pltpu.make_async_copy(out_ref, out_hbm, out_sem)
    copy.start()
    copy.wait()


def energy_kernel(
    stiffness_hbm, centers_hbm, distances_hbm, near_ref, tops_ref, far_hbm,
    stiffness_ref, centers_ref, distances_ref, far_ref, in_sems, far_sem,
):
    together(
        [
            (stiffness_hbm, stiffness_ref),
            (centers_hbm, centers_ref),
            (distances_hbm, distances_ref),
        ],
        in_sems,
    )
    stiffness, centers = stiffness_ref[...] * log2_e, centers_ref[...]
    constant = jnp.sum(-0.5 * stiffness * centers * centers, axis=0, keepdims=True)
    first = lax.broadcasted_iota(jnp.int32, (8, constant.shape[1]), 0) == 0
    constant_rows = jnp.where(first, jnp.broadcast_to(constant, first.shape), 0.0)
    coef_rows = jnp.concatenate([stiffness * centers, -0.5 * stiffness, constant_rows], axis=0).T
    unit_rows = jnp.where(lax.broadcasted_iota(jnp.int32, (8, STEP), 0) == 0, 1.0, 0.0)

    def one(step, to_ref, to):
        start = pl.multiple_of(step * STEP, STEP)
        separations = distances_ref[:, pl.ds(start, STEP)]
        features = jnp.concatenate([separations, separations * separations, unit_rows], axis=0)
        exponents = jnp.dot(
            coef_rows, features, precision=lax.Precision.HIGHEST, preferred_element_type=jnp.float32
        )
        top = jnp.max(exponents, axis=0, keepdims=True)
        to_ref[:, pl.ds(to, STEP)] = exponents - top
        for part in range(STEP // LANES):
            tops_ref[pl.ds(step * (STEP // LANES) + part, 1), :] = top[:, part * LANES : (part + 1) * LANES]

    near_steps = near_ref.shape[1] // STEP
    copy = pltpu.make_async_copy(far_ref, far_hbm, far_sem)
    one(near_steps, far_ref, 0)
    copy.start()

    def near(step, carry):
        one(step, near_ref, pl.multiple_of(step * STEP, STEP))
        return carry

    lax.fori_loop(0, near_steps, near, 0)
    copy.wait()


def denominators(shifted, arrive, parts, tops_ref, out_ref, column_ref, part_ref, row_ref):
    groups = shifted.shape[0]
    most = jnp.max(jnp.max(shifted, axis=0, keepdims=True), axis=1, keepdims=True)
    for group in range(groups):
        spread = jnp.broadcast_to(shifted[group : group + 1] - most, (LANES, LANES))
        column_ref[group * LANES : (group + 1) * LANES, :] = spread.T
    windows = column_ref.shape[0]
    chunks = [slice(start, start + ROWS) for start in range(0, windows, ROWS)]

    def exponents(ref, rows, block):
        return (ref[rows, pl.ds(pl.multiple_of(block * LANES, LANES), LANES)] + column_ref[rows, :]).reshape(
            -1, 8, LANES
        )

    done = 0
    for part, ref in enumerate(parts):
        if part:
            arrive()
        count = ref.shape[1] // LANES

        def one(block, carry, ref=ref, done=done):
            sums = [jnp.sum(jnp.exp2(exponents(ref, rows, block)), axis=0) for rows in chunks]
            part_ref[done + block] = functools.reduce(jnp.add, sums)
            return carry

        lax.fori_loop(0, count, one, 0, unroll=True)
        done += count
    totals = jnp.sum(part_ref[...], axis=1)
    out_ref[...] = jnp.broadcast_to((tops_ref[...] + most + log2(totals))[None], out_ref.shape)

    @pl.when(jnp.min(totals) < least_sum)
    def _():
        done = 0
        for ref in parts:
            count = ref.shape[1] // LANES

            def exact(block, carry, ref=ref, done=done):
                tops = [jnp.max(exponents(ref, rows, block), axis=0) for rows in chunks]
                highest = jnp.max(functools.reduce(jnp.maximum, tops), axis=0, keepdims=True)
                sums = [jnp.sum(jnp.exp2(exponents(ref, rows, block) - highest), axis=0) for rows in chunks]
                total = jnp.sum(functools.reduce(jnp.add, sums), axis=0, keepdims=True)
                row_ref[pl.ds(done + block, 1), :] = highest + log2(total)
                return carry

            lax.fori_loop(0, count, exact, 0)
            done += count
        out_ref[...] = jnp.broadcast_to((tops_ref[...] + most + row_ref[...])[None], out_ref.shape)


def first_kernel(
    lengths_hbm, shared_ref, near_ref, tops_ref, far_hbm, counts_ref, out_ref, far_ref, used_ref,
    column_ref, part_ref, row_ref, lengths_ref, sem, lengths_sem,
):
    copy = pltpu.make_async_copy(far_hbm, far_ref, sem)
    lengths_copy = pltpu.make_async_copy(lengths_hbm, lengths_ref, lengths_sem)
    copy.start()
    lengths_copy.start()
    counts = jnp.sum(shared_ref[...], axis=0)
    counts_ref[...] = counts
    shifted = jnp.where(counts > 0.5, log2(jnp.maximum(counts, 1.0)), floor_value)
    denominators(shifted, copy.wait, (near_ref, far_ref), tops_ref, out_ref, column_ref, part_ref, row_ref)
    lengths_copy.wait()
    own_length = lengths_ref[lax.axis_index("frame")]
    slots = (
        lax.broadcasted_iota(jnp.int32, tops_ref.shape, 0) * LANES
        + lax.broadcasted_iota(jnp.int32, tops_ref.shape, 1)
    )
    used_ref[...] = jnp.where(slots < own_length, tops_ref[...], floor_value)


def next_kernel(shared_ref, counts_ref, near_ref, tops_ref, far_ref, out_ref, column_ref, part_ref, row_ref):
    counts = counts_ref[...]
    free_energy = -log2_sum(shared_ref[...])
    shifted = jnp.where(counts > 0.5, log2(jnp.maximum(counts, 1.0)) + free_energy, floor_value)
    denominators(shifted, lambda: None, (near_ref, far_ref), tops_ref, out_ref, column_ref, part_ref, row_ref)


def window_kernel(shared_ref, near_ref, used_ref, far_ref, out_ref, den_ref, top_ref, sum_ref, row_ref):
    windows, near_blocks, far_blocks = near_ref.shape[0], near_ref.shape[1] // LANES, far_ref.shape[1] // LANES
    groups = windows // LANES
    den_ref[...] = log2_sum(shared_ref[...]) - used_ref[...]

    def exponents(chunk):
        rows = pl.ds(pl.multiple_of(chunk * ROWS, ROWS), ROWS)
        for ref, done in ((near_ref, 0), (far_ref, near_blocks)):
            for block in range(ref.shape[1] // LANES):
                yield ref[rows, block * LANES : (block + 1) * LANES] - den_ref[done + block : done + block + 1, :]

    def one(chunk, carry):
        rows = pl.ds(pl.multiple_of(chunk * ROWS, ROWS), ROWS)
        sum_ref[rows, :] = functools.reduce(jnp.add, (jnp.exp2(each) for each in exponents(chunk)))
        return carry

    lax.fori_loop(0, windows // ROWS, one, 0)
    totals = []
    for group in range(groups):
        total = jnp.sum(sum_ref[group * LANES : (group + 1) * LANES, :].T, axis=0, keepdims=True)
        totals.append(total)
        row_ref[group : group + 1, :] = log2(total)
    out_ref[...] = jnp.broadcast_to(row_ref[...][None], out_ref.shape)
    lowest = jnp.min(functools.reduce(jnp.minimum, totals))
    highest = jnp.max(functools.reduce(jnp.maximum, totals))

    @pl.when(jnp.logical_not(jnp.logical_and(lowest > least_sum, highest < most_sum)))
    def _():
        def exact(chunk, carry):
            rows = pl.ds(pl.multiple_of(chunk * ROWS, ROWS), ROWS)
            top = functools.reduce(jnp.maximum, exponents(chunk))
            top_ref[rows, :] = top
            sum_ref[rows, :] = functools.reduce(jnp.add, (jnp.exp2(each - top) for each in exponents(chunk)))
            return carry

        lax.fori_loop(0, windows // ROWS, exact, 0)
        for group in range(groups):
            rows = slice(group * LANES, (group + 1) * LANES)
            tops, sums = top_ref[rows, :].T, sum_ref[rows, :].T
            top = jnp.max(tops, axis=0, keepdims=True)
            total = jnp.sum(sums * jnp.exp2(tops - top), axis=0, keepdims=True)
            row_ref[group : group + 1, :] = top + log2(total)
        out_ref[...] = jnp.broadcast_to(row_ref[...][None], out_ref.shape)


def exchange(copies, axis):
    return lax.all_to_all(copies, axis, split_axis=0, concat_axis=0, tiled=True)


def on_device(distances, sample_ids, lengths, stiffness, centers):
    windows, capacity = stiffness.shape[0], distances.shape[1]
    groups, blocks, steps = windows // LANES, capacity // LANES, capacity // STEP
    f32, dma = jnp.float32, pltpu.SemaphoreType.DMA
    to_frame = jax.ShapeDtypeStruct((lax.axis_size("frame"), groups, LANES), f32)
    to_win = jax.ShapeDtypeStruct((lax.axis_size("win"), blocks, LANES), f32)
    lengths_here = pltpu.SMEM(lengths.shape, jnp.int32)
    local_counts = pl.pallas_call(
        count_kernel,
        out_shape=to_frame,
        in_specs=[in_hbm] * 2,
        out_specs=in_hbm,
        scratch_shapes=[
            lengths_here,
            pltpu.VMEM((1, capacity), jnp.int32),
            pltpu.VMEM(to_frame.shape, f32),
            dma((2,)),
            dma,
        ],
        name="count_windows",
    )(lengths, sample_ids.reshape(1, capacity))
    shared = exchange(local_counts, "frame")
    far_frames = FAR * STEP
    near_shape = jax.ShapeDtypeStruct((windows, capacity - far_frames), f32)
    far_shape = jax.ShapeDtypeStruct((windows, far_frames), f32)
    tops_shape = jax.ShapeDtypeStruct((blocks, LANES), f32)
    near, tops, far = pl.pallas_call(
        energy_kernel,
        out_shape=(near_shape, tops_shape, pltpu.HBM(far_shape.shape, f32)),
        in_specs=[in_hbm] * 3,
        out_specs=(in_vmem, in_vmem, in_hbm),
        scratch_shapes=[
            pltpu.VMEM((stiffness.shape[1], windows), f32),
            pltpu.VMEM((stiffness.shape[1], windows), f32),
            pltpu.VMEM(distances.shape, f32),
            pltpu.VMEM(far_shape.shape, f32),
            dma((3,)),
            dma,
        ],
        compiler_params=grant,
        cost_estimate=pl.CostEstimate(
            flops=24 * distances.shape[0] * windows * capacity,
            bytes_accessed=4 * windows * capacity,
            transcendentals=0,
        ),
        name="energies",
    )(hbm(stiffness.T), hbm(centers.T), hbm(distances))
    den_scratch = [
        pltpu.VMEM((windows, LANES), f32),
        pltpu.VMEM((blocks, 8, LANES), f32),
        pltpu.VMEM((blocks, LANES), f32),
    ]
    counts, own_den, far, used = pl.pallas_call(
        first_kernel,
        out_shape=(jax.ShapeDtypeStruct((groups, LANES), f32), to_win, far_shape, tops_shape),
        in_specs=[in_hbm, in_vmem, in_vmem, in_vmem, in_hbm],
        out_specs=(in_vmem,) * 4,
        scratch_shapes=[*den_scratch, lengths_here, dma, dma],
        compiler_params=grant,
        name="first_denominators",
    )(hbm(lengths), shared, near, tops, hbm(far))
    for iteration in range(ITERS):
        own_total = pl.pallas_call(
            window_kernel,
            out_shape=to_frame,
            in_specs=[in_vmem] * 4,
            out_specs=in_vmem,
            scratch_shapes=[
                pltpu.VMEM((blocks, LANES), f32),
                pltpu.VMEM((windows, LANES), f32),
                pltpu.VMEM((windows, LANES), f32),
                pltpu.VMEM((groups, LANES), f32),
            ],
            compiler_params=grant,
            name="window_totals",
        )(exchange(own_den, "win"), near, used, far)
        shared = exchange(own_total, "frame")
        if iteration < ITERS - 1:
            own_den = pl.pallas_call(
                next_kernel,
                out_shape=to_win,
                in_specs=[in_vmem] * 5,
                out_specs=in_vmem,
                scratch_shapes=den_scratch,
                compiler_params=grant,
                name="next_denominators",
            )(shared, counts, near, tops, far)
    return (-math.log(2.0) * log2_sum(shared)).reshape(windows)


def solution(mesh):
    return jax.shard_map(
        on_device,
        mesh=mesh,
        in_specs=(P(None, "frame"), P("frame"), P(), P("win", None), P("win", None)),
        out_specs=P("win"),
        check_vma=False,
    )
```

```python
import functools
import math

import jax
import jax.numpy as jnp
from jax import lax
from jax.experimental import pallas as pl
from jax.experimental.pallas import tpu as pltpu
from jax.sharding import PartitionSpec as P


ITERS = 2
LANES = 128
ROWS = 64
STEP = 512

floor_value = -1e30
log2_e = 1.0 / math.log(2.0)
FAR = 1
FIRST = {"frame": 34, "win": 4}
least_sum = 2.0**-80
most_sum = 2.0**100

in_vmem = pl.BlockSpec(memory_space=pltpu.VMEM)
in_hbm = pl.BlockSpec(memory_space=pltpu.HBM)
grant = pltpu.CompilerParams(vmem_limit_bytes=12 << 20)


def hbm(array):
    return pltpu.with_memory_space_constraint(array, pltpu.HBM)


def log2(values):
    return jnp.log(values) * log2_e


def log2_sum(values):
    highest = jnp.max(values, axis=0)
    return highest + log2(jnp.sum(jnp.exp2(values - highest[None]), axis=0))


def together(pairs, sems):
    copies = [pltpu.make_async_copy(*pair, sems.at[place]) for place, pair in enumerate(pairs)]
    for copy in copies:
        copy.start()
    for copy in copies:
        copy.wait()


def count_kernel(lengths_hbm, ids_hbm, out_hbm, lengths_ref, ids_ref, out_ref, in_sems, out_sem):
    together([(lengths_hbm, lengths_ref), (ids_hbm, ids_ref)], in_sems)
    groups = out_ref.shape[1]
    capacity = ids_ref.shape[1]
    own_length = lengths_ref[lax.axis_index("frame")]
    local = ids_ref[...] - lax.axis_index("win") * (groups * LANES)
    slots = lax.broadcasted_iota(jnp.int32, (1, capacity), 1)
    local = jnp.where(slots < own_length, local, -1)
    group = jnp.where(local < 0, -1, lax.shift_right_logical(local, 7))
    place = jnp.bitwise_and(local, LANES - 1)
    in_group = lax.broadcasted_iota(jnp.int32, (8, capacity), 0) == group
    in_place = lax.broadcasted_iota(jnp.int32, (LANES, capacity), 0) == place
    counts = lax.dot_general(
        in_group.astype(jnp.float32).astype(jnp.bfloat16),
        in_place.astype(jnp.float32).astype(jnp.bfloat16),
        (((1,), (1,)), ((), ())),
        preferred_element_type=jnp.float32,
    )
    out_ref[...] = jnp.broadcast_to(counts[None, :groups], out_ref.shape)
    copy = pltpu.make_async_copy(out_ref, out_hbm, out_sem)
    copy.start()
    copy.wait()


def energy_kernel(
    stiffness_hbm, centers_hbm, distances_hbm, near_ref, tops_ref, far_hbm,
    stiffness_ref, centers_ref, distances_ref, far_ref, in_sems, far_sem,
):
    together(
        [
            (stiffness_hbm, stiffness_ref),
            (centers_hbm, centers_ref),
            (distances_hbm, distances_ref),
        ],
        in_sems,
    )
    stiffness, centers = stiffness_ref[...] * log2_e, centers_ref[...]
    constant = jnp.sum(-0.5 * stiffness * centers * centers, axis=0, keepdims=True)
    first = lax.broadcasted_iota(jnp.int32, (8, constant.shape[1]), 0) == 0
    constant_rows = jnp.where(first, jnp.broadcast_to(constant, first.shape), 0.0)
    coef_rows = jnp.concatenate([stiffness * centers, -0.5 * stiffness, constant_rows], axis=0).T
    unit_rows = jnp.where(lax.broadcasted_iota(jnp.int32, (8, STEP), 0) == 0, 1.0, 0.0)

    def one(step, to_ref, to):
        start = pl.multiple_of(step * STEP, STEP)
        separations = distances_ref[:, pl.ds(start, STEP)]
        features = jnp.concatenate([separations, separations * separations, unit_rows], axis=0)
        exponents = jnp.dot(
            coef_rows, features, precision=lax.Precision.HIGHEST, preferred_element_type=jnp.float32
        )
        top = jnp.max(exponents, axis=0, keepdims=True)
        to_ref[:, pl.ds(to, STEP)] = exponents - top
        for part in range(STEP // LANES):
            tops_ref[pl.ds(step * (STEP // LANES) + part, 1), :] = top[:, part * LANES : (part + 1) * LANES]

    near_steps = near_ref.shape[1] // STEP
    copy = pltpu.make_async_copy(far_ref, far_hbm, far_sem)
    one(near_steps, far_ref, 0)
    copy.start()

    def near(step, carry):
        one(step, near_ref, pl.multiple_of(step * STEP, STEP))
        return carry

    lax.fori_loop(0, near_steps, near, 0)
    copy.wait()


def denominators(shifted, arrive, parts, tops_ref, out_ref, column_ref, part_ref, row_ref):
    groups = shifted.shape[0]
    most = jnp.max(jnp.max(shifted, axis=0, keepdims=True), axis=1, keepdims=True)
    for group in range(groups):
        spread = jnp.broadcast_to(shifted[group : group + 1] - most, (LANES, LANES))
        column_ref[group * LANES : (group + 1) * LANES, :] = spread.T
    windows = column_ref.shape[0]
    chunks = [slice(start, start + ROWS) for start in range(0, windows, ROWS)]

    def exponents(ref, rows, block):
        return (ref[rows, pl.ds(pl.multiple_of(block * LANES, LANES), LANES)] + column_ref[rows, :]).reshape(
            -1, 8, LANES
        )

    done = 0
    for part, ref in enumerate(parts):
        if part:
            arrive()
        count = ref.shape[1] // LANES

        def one(block, carry, ref=ref, done=done):
            sums = [jnp.sum(jnp.exp2(exponents(ref, rows, block)), axis=0) for rows in chunks]
            part_ref[done + block] = functools.reduce(jnp.add, sums)
            return carry

        lax.fori_loop(0, count, one, 0, unroll=True)
        done += count
    totals = jnp.sum(part_ref[...], axis=1)
    out_ref[...] = jnp.broadcast_to((tops_ref[...] + most + log2(totals))[None], out_ref.shape)

    @pl.when(jnp.min(totals) < least_sum)
    def _():
        done = 0
        for ref in parts:
            count = ref.shape[1] // LANES

            def exact(block, carry, ref=ref, done=done):
                tops = [jnp.max(exponents(ref, rows, block), axis=0) for rows in chunks]
                highest = jnp.max(functools.reduce(jnp.maximum, tops), axis=0, keepdims=True)
                sums = [jnp.sum(jnp.exp2(exponents(ref, rows, block) - highest), axis=0) for rows in chunks]
                total = jnp.sum(functools.reduce(jnp.add, sums), axis=0, keepdims=True)
                row_ref[pl.ds(done + block, 1), :] = highest + log2(total)
                return carry

            lax.fori_loop(0, count, exact, 0)
            done += count
        out_ref[...] = jnp.broadcast_to((tops_ref[...] + most + row_ref[...])[None], out_ref.shape)


def first_kernel(
    lengths_hbm, shared_ref, near_ref, tops_ref, far_hbm, counts_ref, out_ref, far_ref, used_ref,
    column_ref, part_ref, row_ref, lengths_ref, sem, lengths_sem,
):
    copy = pltpu.make_async_copy(far_hbm, far_ref, sem)
    lengths_copy = pltpu.make_async_copy(lengths_hbm, lengths_ref, lengths_sem)
    copy.start()
    lengths_copy.start()
    counts = jnp.sum(shared_ref[...], axis=0)
    counts_ref[...] = counts
    shifted = jnp.where(counts > 0.5, log2(jnp.maximum(counts, 1.0)), floor_value)
    denominators(shifted, copy.wait, (near_ref, far_ref), tops_ref, out_ref, column_ref, part_ref, row_ref)
    lengths_copy.wait()
    own_length = lengths_ref[lax.axis_index("frame")]
    slots = (
        lax.broadcasted_iota(jnp.int32, tops_ref.shape, 0) * LANES
        + lax.broadcasted_iota(jnp.int32, tops_ref.shape, 1)
    )
    used_ref[...] = jnp.where(slots < own_length, tops_ref[...], floor_value)


def next_kernel(shared_ref, counts_ref, near_ref, tops_ref, far_ref, out_ref, column_ref, part_ref, row_ref):
    counts = counts_ref[...]
    free_energy = -log2_sum(shared_ref[...])
    shifted = jnp.where(counts > 0.5, log2(jnp.maximum(counts, 1.0)) + free_energy, floor_value)
    denominators(shifted, lambda: None, (near_ref, far_ref), tops_ref, out_ref, column_ref, part_ref, row_ref)


def window_kernel(shared_ref, near_ref, used_ref, far_ref, out_ref, den_ref, top_ref, sum_ref, row_ref):
    windows, near_blocks, far_blocks = near_ref.shape[0], near_ref.shape[1] // LANES, far_ref.shape[1] // LANES
    groups = windows // LANES
    den_ref[...] = log2_sum(shared_ref[...]) - used_ref[...]

    def exponents(chunk):
        rows = pl.ds(pl.multiple_of(chunk * ROWS, ROWS), ROWS)
        for ref, done in ((near_ref, 0), (far_ref, near_blocks)):
            for block in range(ref.shape[1] // LANES):
                yield ref[rows, block * LANES : (block + 1) * LANES] - den_ref[done + block : done + block + 1, :]

    def one(chunk, carry):
        rows = pl.ds(pl.multiple_of(chunk * ROWS, ROWS), ROWS)
        sum_ref[rows, :] = functools.reduce(jnp.add, (jnp.exp2(each) for each in exponents(chunk)))
        return carry

    lax.fori_loop(0, windows // ROWS, one, 0)
    totals = []
    for group in range(groups):
        total = jnp.sum(sum_ref[group * LANES : (group + 1) * LANES, :].T, axis=0, keepdims=True)
        totals.append(total)
        row_ref[group : group + 1, :] = log2(total)
    out_ref[...] = jnp.broadcast_to(row_ref[...][None], out_ref.shape)
    lowest = jnp.min(functools.reduce(jnp.minimum, totals))
    highest = jnp.max(functools.reduce(jnp.maximum, totals))

    @pl.when(jnp.logical_not(jnp.logical_and(lowest > least_sum, highest < most_sum)))
    def _():
        def exact(chunk, carry):
            rows = pl.ds(pl.multiple_of(chunk * ROWS, ROWS), ROWS)
            top = functools.reduce(jnp.maximum, exponents(chunk))
            top_ref[rows, :] = top
            sum_ref[rows, :] = functools.reduce(jnp.add, (jnp.exp2(each - top) for each in exponents(chunk)))
            return carry

        lax.fori_loop(0, windows // ROWS, exact, 0)
        for group in range(groups):
            rows = slice(group * LANES, (group + 1) * LANES)
            tops, sums = top_ref[rows, :].T, sum_ref[rows, :].T
            top = jnp.max(tops, axis=0, keepdims=True)
            total = jnp.sum(sums * jnp.exp2(tops - top), axis=0, keepdims=True)
            row_ref[group : group + 1, :] = top + log2(total)
        out_ref[...] = jnp.broadcast_to(row_ref[...][None], out_ref.shape)


def exchange(copies, axis):
    count = lax.axis_size(axis)
    order = [(member + FIRST[axis]) % count for member in range(count)]
    return lax.all_to_all(copies, axis, split_axis=0, concat_axis=0, tiled=True, axis_index_groups=[order])


def on_device(distances, sample_ids, lengths, stiffness, centers):
    windows, capacity = stiffness.shape[0], distances.shape[1]
    groups, blocks, steps = windows // LANES, capacity // LANES, capacity // STEP
    f32, dma = jnp.float32, pltpu.SemaphoreType.DMA
    to_frame = jax.ShapeDtypeStruct((lax.axis_size("frame"), groups, LANES), f32)
    to_win = jax.ShapeDtypeStruct((lax.axis_size("win"), blocks, LANES), f32)
    lengths_here = pltpu.SMEM(lengths.shape, jnp.int32)
    local_counts = pl.pallas_call(
        count_kernel,
        out_shape=to_frame,
        in_specs=[in_hbm] * 2,
        out_specs=in_hbm,
        scratch_shapes=[
            lengths_here,
            pltpu.VMEM((1, capacity), jnp.int32),
            pltpu.VMEM(to_frame.shape, f32),
            dma((2,)),
            dma,
        ],
        name="count_windows",
    )(lengths, sample_ids.reshape(1, capacity))
    shared = exchange(local_counts, "frame")
    far_frames = FAR * STEP
    near_shape = jax.ShapeDtypeStruct((windows, capacity - far_frames), f32)
    far_shape = jax.ShapeDtypeStruct((windows, far_frames), f32)
    tops_shape = jax.ShapeDtypeStruct((blocks, LANES), f32)
    near, tops, far = pl.pallas_call(
        energy_kernel,
        out_shape=(near_shape, tops_shape, pltpu.HBM(far_shape.shape, f32)),
        in_specs=[in_hbm] * 3,
        out_specs=(in_vmem, in_vmem, in_hbm),
        scratch_shapes=[
            pltpu.VMEM((stiffness.shape[1], windows), f32),
            pltpu.VMEM((stiffness.shape[1], windows), f32),
            pltpu.VMEM(distances.shape, f32),
            pltpu.VMEM(far_shape.shape, f32),
            dma((3,)),
            dma,
        ],
        compiler_params=grant,
        cost_estimate=pl.CostEstimate(
            flops=24 * distances.shape[0] * windows * capacity,
            bytes_accessed=4 * windows * capacity,
            transcendentals=0,
        ),
        name="energies",
    )(hbm(stiffness.T), hbm(centers.T), hbm(distances))
    den_scratch = [
        pltpu.VMEM((windows, LANES), f32),
        pltpu.VMEM((blocks, 8, LANES), f32),
        pltpu.VMEM((blocks, LANES), f32),
    ]
    counts, own_den, far, used = pl.pallas_call(
        first_kernel,
        out_shape=(jax.ShapeDtypeStruct((groups, LANES), f32), to_win, far_shape, tops_shape),
        in_specs=[in_hbm, in_vmem, in_vmem, in_vmem, in_hbm],
        out_specs=(in_vmem,) * 4,
        scratch_shapes=[*den_scratch, lengths_here, dma, dma],
        compiler_params=grant,
        name="first_denominators",
    )(hbm(lengths), shared, near, tops, hbm(far))
    for iteration in range(ITERS):
        own_total = pl.pallas_call(
            window_kernel,
            out_shape=to_frame,
            in_specs=[in_vmem] * 4,
            out_specs=in_vmem,
            scratch_shapes=[
                pltpu.VMEM((blocks, LANES), f32),
                pltpu.VMEM((windows, LANES), f32),
                pltpu.VMEM((windows, LANES), f32),
                pltpu.VMEM((groups, LANES), f32),
            ],
            compiler_params=grant,
            name="window_totals",
        )(exchange(own_den, "win"), near, used, far)
        shared = exchange(own_total, "frame")
        if iteration < ITERS - 1:
            own_den = pl.pallas_call(
                next_kernel,
                out_shape=to_win,
                in_specs=[in_vmem] * 5,
                out_specs=in_vmem,
                scratch_shapes=den_scratch,
                compiler_params=grant,
                name="next_denominators",
            )(shared, counts, near, tops, far)
    return (-math.log(2.0) * log2_sum(shared)).reshape(windows)


def solution(mesh):
    return jax.shard_map(
        on_device,
        mesh=mesh,
        in_specs=(P(None, "frame"), P("frame"), P(), P("win", None), P("win", None)),
        out_specs=P("win"),
        check_vma=False,
    )
```

```python
import functools
import math

import jax
import jax.numpy as jnp
from jax import lax
from jax.experimental import pallas as pl
from jax.experimental.pallas import tpu as pltpu
from jax.sharding import PartitionSpec as P


ITERS = 2
LANES = 128
ROWS = 64
STEP = 512

floor_value = -1e30
log2_e = 1.0 / math.log(2.0)
FAR = 384
FIRST = {"frame": 34, "win": 4}
least_sum = 2.0**-80
most_sum = 2.0**100

in_vmem = pl.BlockSpec(memory_space=pltpu.VMEM)
in_hbm = pl.BlockSpec(memory_space=pltpu.HBM)
grant = pltpu.CompilerParams(vmem_limit_bytes=12 << 20)


def hbm(array):
    return pltpu.with_memory_space_constraint(array, pltpu.HBM)


def log2(values):
    return jnp.log(values) * log2_e


def log2_sum(values):
    highest = jnp.max(values, axis=0)
    return highest + log2(jnp.sum(jnp.exp2(values - highest[None]), axis=0))


def together(pairs, sems):
    copies = [pltpu.make_async_copy(*pair, sems.at[place]) for place, pair in enumerate(pairs)]
    for copy in copies:
        copy.start()
    for copy in copies:
        copy.wait()


def count_kernel(lengths_hbm, ids_hbm, out_hbm, lengths_ref, ids_ref, out_ref, in_sems, out_sem):
    together([(lengths_hbm, lengths_ref), (ids_hbm, ids_ref)], in_sems)
    groups = out_ref.shape[1]
    capacity = ids_ref.shape[1]
    own_length = lengths_ref[lax.axis_index("frame")]
    local = ids_ref[...] - lax.axis_index("win") * (groups * LANES)
    slots = lax.broadcasted_iota(jnp.int32, (1, capacity), 1)
    local = jnp.where(slots < own_length, local, -1)
    group = jnp.where(local < 0, -1, lax.shift_right_logical(local, 7))
    place = jnp.bitwise_and(local, LANES - 1)
    in_group = lax.broadcasted_iota(jnp.int32, (8, capacity), 0) == group
    in_place = lax.broadcasted_iota(jnp.int32, (LANES, capacity), 0) == place
    counts = lax.dot_general(
        in_group.astype(jnp.float32).astype(jnp.bfloat16),
        in_place.astype(jnp.float32).astype(jnp.bfloat16),
        (((1,), (1,)), ((), ())),
        preferred_element_type=jnp.float32,
    )
    out_ref[...] = jnp.broadcast_to(counts[None, :groups], out_ref.shape)
    copy = pltpu.make_async_copy(out_ref, out_hbm, out_sem)
    copy.start()
    copy.wait()


def energy_kernel(
    stiffness_hbm, centers_hbm, distances_hbm, near_ref, tops_ref, far_hbm,
    stiffness_ref, centers_ref, distances_ref, far_ref, in_sems, far_sem,
):
    together(
        [
            (stiffness_hbm, stiffness_ref),
            (centers_hbm, centers_ref),
            (distances_hbm, distances_ref),
        ],
        in_sems,
    )
    stiffness, centers = stiffness_ref[...] * log2_e, centers_ref[...]
    constant = jnp.sum(-0.5 * stiffness * centers * centers, axis=0, keepdims=True)
    first = lax.broadcasted_iota(jnp.int32, (8, constant.shape[1]), 0) == 0
    constant_rows = jnp.where(first, jnp.broadcast_to(constant, first.shape), 0.0)
    coef_rows = jnp.concatenate([stiffness * centers, -0.5 * stiffness, constant_rows], axis=0).T

    def one(start, size, to_ref, to):
        unit_rows = jnp.where(lax.broadcasted_iota(jnp.int32, (8, size), 0) == 0, 1.0, 0.0)
        separations = distances_ref[:, pl.ds(start, size)]
        features = jnp.concatenate([separations, separations * separations, unit_rows], axis=0)
        exponents = jnp.dot(
            coef_rows, features, precision=lax.Precision.HIGHEST, preferred_element_type=jnp.float32
        )
        top = jnp.max(exponents, axis=0, keepdims=True)
        to_ref[:, pl.ds(to, size)] = exponents - top
        for part in range(size // LANES):
            tops_ref[pl.ds(start // LANES + part, 1), :] = top[:, part * LANES : (part + 1) * LANES]

    near_frames, far_frames = near_ref.shape[1], far_ref.shape[1]
    copy = pltpu.make_async_copy(far_ref, far_hbm, far_sem)
    one(near_frames, far_frames, far_ref, 0)
    copy.start()

    def near(step, carry):
        start = pl.multiple_of(step * STEP, STEP)
        one(start, STEP, near_ref, start)
        return carry

    lax.fori_loop(0, near_frames // STEP, near, 0)
    rest = near_frames % STEP
    if rest:
        one(near_frames - rest, rest, near_ref, near_frames - rest)
    copy.wait()


def denominators(shifted, arrive, parts, tops_ref, out_ref, column_ref, part_ref, row_ref):
    groups = shifted.shape[0]
    most = jnp.max(jnp.max(shifted, axis=0, keepdims=True), axis=1, keepdims=True)
    for group in range(groups):
        spread = jnp.broadcast_to(shifted[group : group + 1] - most, (LANES, LANES))
        column_ref[group * LANES : (group + 1) * LANES, :] = spread.T
    windows = column_ref.shape[0]
    chunks = [slice(start, start + ROWS) for start in range(0, windows, ROWS)]

    def exponents(ref, rows, block):
        return (ref[rows, pl.ds(pl.multiple_of(block * LANES, LANES), LANES)] + column_ref[rows, :]).reshape(
            -1, 8, LANES
        )

    done = 0
    for part, ref in enumerate(parts):
        if part:
            arrive()
        count = ref.shape[1] // LANES

        def one(block, carry, ref=ref, done=done):
            sums = [jnp.sum(jnp.exp2(exponents(ref, rows, block)), axis=0) for rows in chunks]
            part_ref[done + block] = functools.reduce(jnp.add, sums)
            return carry

        lax.fori_loop(0, count, one, 0, unroll=True)
        done += count
    totals = jnp.sum(part_ref[...], axis=1)
    out_ref[...] = jnp.broadcast_to((tops_ref[...] + most + log2(totals))[None], out_ref.shape)

    @pl.when(jnp.min(totals) < least_sum)
    def _():
        done = 0
        for ref in parts:
            count = ref.shape[1] // LANES

            def exact(block, carry, ref=ref, done=done):
                tops = [jnp.max(exponents(ref, rows, block), axis=0) for rows in chunks]
                highest = jnp.max(functools.reduce(jnp.maximum, tops), axis=0, keepdims=True)
                sums = [jnp.sum(jnp.exp2(exponents(ref, rows, block) - highest), axis=0) for rows in chunks]
                total = jnp.sum(functools.reduce(jnp.add, sums), axis=0, keepdims=True)
                row_ref[pl.ds(done + block, 1), :] = highest + log2(total)
                return carry

            lax.fori_loop(0, count, exact, 0)
            done += count
        out_ref[...] = jnp.broadcast_to((tops_ref[...] + most + row_ref[...])[None], out_ref.shape)


def first_kernel(
    lengths_hbm, shared_ref, near_ref, tops_ref, far_hbm, counts_ref, out_ref, far_ref, used_ref,
    column_ref, part_ref, row_ref, lengths_ref, sem, lengths_sem,
):
    copy = pltpu.make_async_copy(far_hbm, far_ref, sem)
    lengths_copy = pltpu.make_async_copy(lengths_hbm, lengths_ref, lengths_sem)
    copy.start()
    lengths_copy.start()
    counts = jnp.sum(shared_ref[...], axis=0)
    counts_ref[...] = counts
    shifted = jnp.where(counts > 0.5, log2(jnp.maximum(counts, 1.0)), floor_value)
    denominators(shifted, copy.wait, (near_ref, far_ref), tops_ref, out_ref, column_ref, part_ref, row_ref)
    lengths_copy.wait()
    own_length = lengths_ref[lax.axis_index("frame")]
    slots = (
        lax.broadcasted_iota(jnp.int32, tops_ref.shape, 0) * LANES
        + lax.broadcasted_iota(jnp.int32, tops_ref.shape, 1)
    )
    used_ref[...] = jnp.where(slots < own_length, tops_ref[...], floor_value)


def next_kernel(shared_ref, counts_ref, near_ref, tops_ref, far_ref, out_ref, column_ref, part_ref, row_ref):
    counts = counts_ref[...]
    free_energy = -log2_sum(shared_ref[...])
    shifted = jnp.where(counts > 0.5, log2(jnp.maximum(counts, 1.0)) + free_energy, floor_value)
    denominators(shifted, lambda: None, (near_ref, far_ref), tops_ref, out_ref, column_ref, part_ref, row_ref)


def window_kernel(shared_ref, near_ref, used_ref, far_ref, out_ref, den_ref, top_ref, sum_ref, row_ref):
    windows, near_blocks, far_blocks = near_ref.shape[0], near_ref.shape[1] // LANES, far_ref.shape[1] // LANES
    groups = windows // LANES
    den_ref[...] = log2_sum(shared_ref[...]) - used_ref[...]

    def exponents(chunk):
        rows = pl.ds(pl.multiple_of(chunk * ROWS, ROWS), ROWS)
        for ref, done in ((near_ref, 0), (far_ref, near_blocks)):
            for block in range(ref.shape[1] // LANES):
                yield ref[rows, block * LANES : (block + 1) * LANES] - den_ref[done + block : done + block + 1, :]

    def one(chunk, carry):
        rows = pl.ds(pl.multiple_of(chunk * ROWS, ROWS), ROWS)
        sum_ref[rows, :] = functools.reduce(jnp.add, (jnp.exp2(each) for each in exponents(chunk)))
        return carry

    lax.fori_loop(0, windows // ROWS, one, 0)
    totals = []
    for group in range(groups):
        total = jnp.sum(sum_ref[group * LANES : (group + 1) * LANES, :].T, axis=0, keepdims=True)
        totals.append(total)
        row_ref[group : group + 1, :] = log2(total)
    out_ref[...] = jnp.broadcast_to(row_ref[...][None], out_ref.shape)
    lowest = jnp.min(functools.reduce(jnp.minimum, totals))
    highest = jnp.max(functools.reduce(jnp.maximum, totals))

    @pl.when(jnp.logical_not(jnp.logical_and(lowest > least_sum, highest < most_sum)))
    def _():
        def exact(chunk, carry):
            rows = pl.ds(pl.multiple_of(chunk * ROWS, ROWS), ROWS)
            top = functools.reduce(jnp.maximum, exponents(chunk))
            top_ref[rows, :] = top
            sum_ref[rows, :] = functools.reduce(jnp.add, (jnp.exp2(each - top) for each in exponents(chunk)))
            return carry

        lax.fori_loop(0, windows // ROWS, exact, 0)
        for group in range(groups):
            rows = slice(group * LANES, (group + 1) * LANES)
            tops, sums = top_ref[rows, :].T, sum_ref[rows, :].T
            top = jnp.max(tops, axis=0, keepdims=True)
            total = jnp.sum(sums * jnp.exp2(tops - top), axis=0, keepdims=True)
            row_ref[group : group + 1, :] = top + log2(total)
        out_ref[...] = jnp.broadcast_to(row_ref[...][None], out_ref.shape)


def last_kernel(shared_ref, out_ref):
    out_ref[...] = -math.log(2.0) * log2_sum(shared_ref[...])


def exchange(copies, axis):
    count = lax.axis_size(axis)
    order = [(member + FIRST[axis]) % count for member in range(count)]
    return lax.all_to_all(copies, axis, split_axis=0, concat_axis=0, tiled=True, axis_index_groups=[order])


def on_device(distances, sample_ids, lengths, stiffness, centers):
    windows, capacity = stiffness.shape[0], distances.shape[1]
    groups, blocks = windows // LANES, capacity // LANES
    f32, dma = jnp.float32, pltpu.SemaphoreType.DMA
    to_frame = jax.ShapeDtypeStruct((lax.axis_size("frame"), groups, LANES), f32)
    to_win = jax.ShapeDtypeStruct((lax.axis_size("win"), blocks, LANES), f32)
    lengths_here = pltpu.SMEM(lengths.shape, jnp.int32)
    local_counts = pl.pallas_call(
        count_kernel,
        out_shape=to_frame,
        in_specs=[in_hbm] * 2,
        out_specs=in_hbm,
        scratch_shapes=[
            lengths_here,
            pltpu.VMEM((1, capacity), jnp.int32),
            pltpu.VMEM(to_frame.shape, f32),
            dma((2,)),
            dma,
        ],
        name="count_windows",
    )(lengths, sample_ids.reshape(1, capacity))
    shared = exchange(local_counts, "frame")
    near_shape = jax.ShapeDtypeStruct((windows, capacity - FAR), f32)
    far_shape = jax.ShapeDtypeStruct((windows, FAR), f32)
    tops_shape = jax.ShapeDtypeStruct((blocks, LANES), f32)
    near, tops, far = pl.pallas_call(
        energy_kernel,
        out_shape=(near_shape, tops_shape, pltpu.HBM(far_shape.shape, f32)),
        in_specs=[in_hbm] * 3,
        out_specs=(in_vmem, in_vmem, in_hbm),
        scratch_shapes=[
            pltpu.VMEM((stiffness.shape[1], windows), f32),
            pltpu.VMEM((stiffness.shape[1], windows), f32),
            pltpu.VMEM(distances.shape, f32),
            pltpu.VMEM(far_shape.shape, f32),
            dma((3,)),
            dma,
        ],
        compiler_params=grant,
        cost_estimate=pl.CostEstimate(
            flops=24 * distances.shape[0] * windows * capacity,
            bytes_accessed=4 * windows * capacity,
            transcendentals=0,
        ),
        name="energies",
    )(hbm(stiffness.T), hbm(centers.T), hbm(distances))
    den_scratch = [
        pltpu.VMEM((windows, LANES), f32),
        pltpu.VMEM((blocks, 8, LANES), f32),
        pltpu.VMEM((blocks, LANES), f32),
    ]
    counts, own_den, far, used = pl.pallas_call(
        first_kernel,
        out_shape=(jax.ShapeDtypeStruct((groups, LANES), f32), to_win, far_shape, tops_shape),
        in_specs=[in_hbm, in_vmem, in_vmem, in_vmem, in_hbm],
        out_specs=(in_vmem,) * 4,
        scratch_shapes=[*den_scratch, lengths_here, dma, dma],
        compiler_params=grant,
        name="first_denominators",
    )(hbm(lengths), shared, near, tops, hbm(far))
    for iteration in range(ITERS):
        own_total = pl.pallas_call(
            window_kernel,
            out_shape=to_frame,
            in_specs=[in_vmem] * 4,
            out_specs=in_vmem,
            scratch_shapes=[
                pltpu.VMEM((blocks, LANES), f32),
                pltpu.VMEM((windows, LANES), f32),
                pltpu.VMEM((windows, LANES), f32),
                pltpu.VMEM((groups, LANES), f32),
            ],
            compiler_params=grant,
            name="window_totals",
        )(exchange(own_den, "win"), near, used, far)
        shared = exchange(own_total, "frame")
        if iteration < ITERS - 1:
            own_den = pl.pallas_call(
                next_kernel,
                out_shape=to_win,
                in_specs=[in_vmem] * 5,
                out_specs=in_vmem,
                scratch_shapes=den_scratch,
                compiler_params=grant,
                name="next_denominators",
            )(shared, counts, near, tops, far)
    free_energy = pl.pallas_call(
        last_kernel,
        out_shape=jax.ShapeDtypeStruct((groups, LANES), f32),
        in_specs=[in_vmem],
        out_specs=in_vmem,
        compiler_params=grant,
        name="free_energies",
    )(shared)
    return free_energy.reshape(windows)


def solution(mesh):
    return jax.shard_map(
        on_device,
        mesh=mesh,
        in_specs=(P(None, "frame"), P("frame"), P(), P("win", None), P("win", None)),
        out_specs=P("win"),
        check_vma=False,
    )
```

```python
import functools
import math

import jax
import jax.numpy as jnp
from jax import lax
from jax.experimental import pallas as pl
from jax.experimental.pallas import tpu as pltpu
from jax.sharding import PartitionSpec as P


ITERS = 2
LANES = 128
ROWS = 64
STEP = 512

floor_value = -1e30
log2_e = 1.0 / math.log(2.0)
FAR = 384
FIRST = {"frame": 34, "win": 4}
least_sum = 2.0**-85
most_rate = 2.0**99

in_vmem = pl.BlockSpec(memory_space=pltpu.VMEM)
in_hbm = pl.BlockSpec(memory_space=pltpu.HBM)
grant = pltpu.CompilerParams(vmem_limit_bytes=12 << 20)


def hbm(array):
    return pltpu.with_memory_space_constraint(array, pltpu.HBM)


def log2(values):
    return jnp.log(values) * log2_e


def log2_sum(values):
    highest = jnp.max(values, axis=0)
    return highest + log2(jnp.sum(jnp.exp2(values - highest[None]), axis=0))


def together(pairs, sems):
    copies = [pltpu.make_async_copy(*pair, sems.at[place]) for place, pair in enumerate(pairs)]
    for copy in copies:
        copy.start()
    for copy in copies:
        copy.wait()


def count_kernel(lengths_hbm, ids_hbm, out_hbm, lengths_ref, ids_ref, out_ref, in_sems, out_sem):
    together([(lengths_hbm, lengths_ref), (ids_hbm, ids_ref)], in_sems)
    groups = out_ref.shape[1]
    capacity = ids_ref.shape[1]
    own_length = lengths_ref[lax.axis_index("frame")]
    local = ids_ref[...] - lax.axis_index("win") * (groups * LANES)
    slots = lax.broadcasted_iota(jnp.int32, (1, capacity), 1)
    local = jnp.where(slots < own_length, local, -1)
    group = jnp.where(local < 0, -1, lax.shift_right_logical(local, 7))
    place = jnp.bitwise_and(local, LANES - 1)
    in_group = lax.broadcasted_iota(jnp.int32, (8, capacity), 0) == group
    in_place = lax.broadcasted_iota(jnp.int32, (LANES, capacity), 0) == place
    counts = lax.dot_general(
        in_group.astype(jnp.float32).astype(jnp.bfloat16),
        in_place.astype(jnp.float32).astype(jnp.bfloat16),
        (((1,), (1,)), ((), ())),
        preferred_element_type=jnp.float32,
    )
    out_ref[...] = jnp.broadcast_to(counts[None, :groups], out_ref.shape)
    copy = pltpu.make_async_copy(out_ref, out_hbm, out_sem)
    copy.start()
    copy.wait()


def energy_kernel(
    stiffness_hbm, centers_hbm, distances_hbm, near_ref, tops_ref, far_hbm, fall_hbm,
    stiffness_ref, centers_ref, distances_ref, far_ref, fall_ref, in_sems, far_sem, fall_sems,
):
    together(
        [
            (stiffness_hbm, stiffness_ref),
            (centers_hbm, centers_ref),
            (distances_hbm, distances_ref),
        ],
        in_sems,
    )
    stiffness, centers = stiffness_ref[...] * log2_e, centers_ref[...]
    constant = jnp.sum(-0.5 * stiffness * centers * centers, axis=0, keepdims=True)
    first = lax.broadcasted_iota(jnp.int32, (8, constant.shape[1]), 0) == 0
    constant_rows = jnp.where(first, jnp.broadcast_to(constant, first.shape), 0.0)
    coef_rows = jnp.concatenate([stiffness * centers, -0.5 * stiffness, constant_rows], axis=0).T

    def send(index, start, size):
        columns = pl.ds(start, size)
        return pltpu.make_async_copy(fall_ref.at[:, columns], fall_hbm.at[:, columns], fall_sems.at[index])

    def one(index, start, size, to_ref, to):
        unit_rows = jnp.where(lax.broadcasted_iota(jnp.int32, (8, size), 0) == 0, 1.0, 0.0)
        separations = distances_ref[:, pl.ds(start, size)]
        features = jnp.concatenate([separations, separations * separations, unit_rows], axis=0)
        exponents = jnp.dot(
            coef_rows, features, precision=lax.Precision.HIGHEST, preferred_element_type=jnp.float32
        )
        top = jnp.max(exponents, axis=0, keepdims=True)
        fall = exponents - top
        fall_ref[:, pl.ds(start, size)] = fall
        send(index, start, size).start()
        to_ref[:, pl.ds(to, size)] = jnp.exp2(fall)
        for part in range(size // LANES):
            tops_ref[pl.ds(start // LANES + part, 1), :] = top[:, part * LANES : (part + 1) * LANES]

    near_frames, far_frames = near_ref.shape[1], far_ref.shape[1]
    copy = pltpu.make_async_copy(far_ref, far_hbm, far_sem)
    steps, rest = near_frames // STEP, near_frames % STEP
    one(steps, near_frames, far_frames, far_ref, 0)
    copy.start()

    def near(step, carry):
        start = pl.multiple_of(step * STEP, STEP)
        one(step, start, STEP, near_ref, start)
        return carry

    lax.fori_loop(0, steps, near, 0)
    if rest:
        one(steps + 1, near_frames - rest, rest, near_ref, near_frames - rest)
        send(steps + 1, near_frames - rest, rest).wait()
    copy.wait()
    send(steps, near_frames, far_frames).wait()
    for step in range(steps):
        send(step, step * STEP, STEP).wait()


def spread(row, to_ref):
    for group in range(row.shape[0]):
        lanes = jnp.broadcast_to(row[group : group + 1], (LANES, LANES))
        to_ref[group * LANES : (group + 1) * LANES, :] = lanes.T


def denominators(shifted, arrive, parts, fall_hbm, tops_ref, out_ref, scratch):
    column_ref, part_ref, row_ref, fall_ref, fall_sem = scratch
    most = jnp.max(jnp.max(shifted, axis=0, keepdims=True), axis=1, keepdims=True)
    spread(jnp.exp2(shifted - most), column_ref)
    windows = column_ref.shape[0]
    chunks = [slice(start, start + ROWS) for start in range(0, windows, ROWS)]

    def columns(block):
        return pl.ds(pl.multiple_of(block * LANES, LANES), LANES)

    def fold(values):
        return values.reshape(-1, 8, LANES)

    done = 0
    for part, ref in enumerate(parts):
        if part:
            arrive()
        count = ref.shape[1] // LANES

        def one(block, carry, ref=ref, done=done):
            sums = [jnp.sum(fold(ref[rows, columns(block)] * column_ref[rows, :]), axis=0) for rows in chunks]
            part_ref[done + block] = functools.reduce(jnp.add, sums)
            return carry

        lax.fori_loop(0, count, one, 0, unroll=True)
        done += count
    totals = jnp.sum(part_ref[...], axis=1)
    out_ref[...] = jnp.broadcast_to((tops_ref[...] + most + log2(totals))[None], out_ref.shape)

    @pl.when(jnp.min(totals) < least_sum)
    def _():
        copy = pltpu.make_async_copy(fall_hbm, fall_ref, fall_sem)
        copy.start()
        spread(shifted - most, column_ref)
        copy.wait()

        def exponents(rows, block):
            return fold(fall_ref[rows, columns(block)] + column_ref[rows, :])

        def exact(block, carry):
            tops = [jnp.max(exponents(rows, block), axis=0) for rows in chunks]
            highest = jnp.max(functools.reduce(jnp.maximum, tops), axis=0, keepdims=True)
            sums = [jnp.sum(jnp.exp2(exponents(rows, block) - highest), axis=0) for rows in chunks]
            total = jnp.sum(functools.reduce(jnp.add, sums), axis=0, keepdims=True)
            row_ref[pl.ds(block, 1), :] = highest + log2(total)
            return carry

        lax.fori_loop(0, row_ref.shape[0], exact, 0)
        out_ref[...] = jnp.broadcast_to((tops_ref[...] + most + row_ref[...])[None], out_ref.shape)


def first_kernel(
    lengths_hbm, shared_ref, near_ref, tops_ref, far_hbm, fall_hbm, counts_ref, out_ref, far_ref, used_ref,
    lengths_ref, sem, lengths_sem, *scratch,
):
    copy = pltpu.make_async_copy(far_hbm, far_ref, sem)
    lengths_copy = pltpu.make_async_copy(lengths_hbm, lengths_ref, lengths_sem)
    copy.start()
    lengths_copy.start()
    counts = jnp.sum(shared_ref[...], axis=0)
    counts_ref[...] = counts
    shifted = jnp.where(counts > 0.5, log2(jnp.maximum(counts, 1.0)), floor_value)
    denominators(shifted, copy.wait, (near_ref, far_ref), fall_hbm, tops_ref, out_ref, scratch)
    lengths_copy.wait()
    own_length = lengths_ref[lax.axis_index("frame")]
    slots = (
        lax.broadcasted_iota(jnp.int32, tops_ref.shape, 0) * LANES
        + lax.broadcasted_iota(jnp.int32, tops_ref.shape, 1)
    )
    used_ref[...] = jnp.where(slots < own_length, tops_ref[...], floor_value)


def next_kernel(shared_ref, counts_ref, near_ref, tops_ref, far_ref, fall_hbm, out_ref, *scratch):
    counts = counts_ref[...]
    free_energy = -log2_sum(shared_ref[...])
    shifted = jnp.where(counts > 0.5, log2(jnp.maximum(counts, 1.0)) + free_energy, floor_value)
    denominators(shifted, lambda: None, (near_ref, far_ref), fall_hbm, tops_ref, out_ref, scratch)


def window_kernel(
    shared_ref, near_ref, used_ref, far_ref, fall_hbm, out_ref, den_ref, rate_ref, top_ref, sum_ref, row_ref, fall_ref, fall_sem
):
    windows, blocks = near_ref.shape[0], den_ref.shape[0]
    groups = windows // LANES
    den = log2_sum(shared_ref[...]) - used_ref[...]
    den_ref[...] = den
    rates = jnp.exp2(-jnp.maximum(den, -100.0))
    rate_ref[...] = rates
    fastest = jnp.max(rates)

    def rows_of(chunk):
        return pl.ds(pl.multiple_of(chunk * ROWS, ROWS), ROWS)

    def one(chunk, carry):
        rows = rows_of(chunk)
        terms = (
            ref[rows, block * LANES : (block + 1) * LANES] * rate_ref[done + block : done + block + 1, :]
            for ref, done in ((near_ref, 0), (far_ref, near_ref.shape[1] // LANES))
            for block in range(ref.shape[1] // LANES)
        )
        sum_ref[rows, :] = functools.reduce(jnp.add, terms)
        return carry

    lax.fori_loop(0, windows // ROWS, one, 0)
    totals = []
    for group in range(groups):
        total = jnp.sum(sum_ref[group * LANES : (group + 1) * LANES, :].T, axis=0, keepdims=True)
        totals.append(total)
        row_ref[group : group + 1, :] = log2(total)
    out_ref[...] = jnp.broadcast_to(row_ref[...][None], out_ref.shape)
    lowest = jnp.min(functools.reduce(jnp.minimum, totals))
    in_range = jnp.logical_and(lowest > least_sum * jnp.maximum(fastest, 1.0), fastest < most_rate)

    @pl.when(jnp.logical_not(in_range))
    def _():
        copy = pltpu.make_async_copy(fall_hbm, fall_ref, fall_sem)
        copy.start()
        copy.wait()

        def exponents(rows, block):
            return fall_ref[rows, block * LANES : (block + 1) * LANES] - den_ref[block : block + 1, :]

        def exact(chunk, carry):
            rows = rows_of(chunk)
            top = functools.reduce(jnp.maximum, (exponents(rows, block) for block in range(blocks)))
            top_ref[rows, :] = top
            sum_ref[rows, :] = functools.reduce(
                jnp.add, (jnp.exp2(exponents(rows, block) - top) for block in range(blocks))
            )
            return carry

        lax.fori_loop(0, windows // ROWS, exact, 0)
        for group in range(groups):
            rows = slice(group * LANES, (group + 1) * LANES)
            tops, sums = top_ref[rows, :].T, sum_ref[rows, :].T
            top = jnp.max(tops, axis=0, keepdims=True)
            total = jnp.sum(sums * jnp.exp2(tops - top), axis=0, keepdims=True)
            row_ref[group : group + 1, :] = top + log2(total)
        out_ref[...] = jnp.broadcast_to(row_ref[...][None], out_ref.shape)


def last_kernel(shared_ref, out_ref):
    out_ref[...] = -math.log(2.0) * log2_sum(shared_ref[...])


def exchange(copies, axis):
    count = lax.axis_size(axis)
    order = [(member + FIRST[axis]) % count for member in range(count)]
    return lax.all_to_all(copies, axis, split_axis=0, concat_axis=0, tiled=True, axis_index_groups=[order])


def on_device(distances, sample_ids, lengths, stiffness, centers):
    windows, capacity = stiffness.shape[0], distances.shape[1]
    groups, blocks = windows // LANES, capacity // LANES
    f32, dma = jnp.float32, pltpu.SemaphoreType.DMA
    to_frame = jax.ShapeDtypeStruct((lax.axis_size("frame"), groups, LANES), f32)
    to_win = jax.ShapeDtypeStruct((lax.axis_size("win"), blocks, LANES), f32)
    lengths_here = pltpu.SMEM(lengths.shape, jnp.int32)
    local_counts = pl.pallas_call(
        count_kernel,
        out_shape=to_frame,
        in_specs=[in_hbm] * 2,
        out_specs=in_hbm,
        scratch_shapes=[
            lengths_here,
            pltpu.VMEM((1, capacity), jnp.int32),
            pltpu.VMEM(to_frame.shape, f32),
            dma((2,)),
            dma,
        ],
        name="count_windows",
    )(lengths, sample_ids.reshape(1, capacity))
    shared = exchange(local_counts, "frame")
    near_shape = jax.ShapeDtypeStruct((windows, capacity - FAR), f32)
    far_shape = jax.ShapeDtypeStruct((windows, FAR), f32)
    tops_shape = jax.ShapeDtypeStruct((blocks, LANES), f32)
    fall_here = [pltpu.VMEM((windows, capacity), f32), dma]
    near, tops, far, fall = pl.pallas_call(
        energy_kernel,
        out_shape=(
            near_shape,
            tops_shape,
            pltpu.HBM(far_shape.shape, f32),
            pltpu.HBM((windows, capacity), f32),
        ),
        in_specs=[in_hbm] * 3,
        out_specs=(in_vmem, in_vmem, in_hbm, in_hbm),
        scratch_shapes=[
            pltpu.VMEM((stiffness.shape[1], windows), f32),
            pltpu.VMEM((stiffness.shape[1], windows), f32),
            pltpu.VMEM(distances.shape, f32),
            pltpu.VMEM(far_shape.shape, f32),
            pltpu.VMEM((windows, capacity), f32),
            dma((3,)),
            dma,
            dma((capacity // STEP + 1,)),
        ],
        compiler_params=grant,
        cost_estimate=pl.CostEstimate(
            flops=24 * distances.shape[0] * windows * capacity,
            bytes_accessed=4 * windows * capacity,
            transcendentals=0,
        ),
        name="energies",
    )(hbm(stiffness.T), hbm(centers.T), hbm(distances))
    fall = hbm(fall)
    den_scratch = [
        pltpu.VMEM((windows, LANES), f32),
        pltpu.VMEM((blocks, 8, LANES), f32),
        pltpu.VMEM((blocks, LANES), f32),
        *fall_here,
    ]
    counts, own_den, far, used = pl.pallas_call(
        first_kernel,
        out_shape=(jax.ShapeDtypeStruct((groups, LANES), f32), to_win, far_shape, tops_shape),
        in_specs=[in_hbm, in_vmem, in_vmem, in_vmem, in_hbm, in_hbm],
        out_specs=(in_vmem,) * 4,
        scratch_shapes=[lengths_here, dma, dma, *den_scratch],
        compiler_params=grant,
        name="first_denominators",
    )(hbm(lengths), shared, near, tops, hbm(far), fall)
    for iteration in range(ITERS):
        own_total = pl.pallas_call(
            window_kernel,
            out_shape=to_frame,
            in_specs=[in_vmem] * 4 + [in_hbm],
            out_specs=in_vmem,
            scratch_shapes=[
                pltpu.VMEM((blocks, LANES), f32),
                pltpu.VMEM((blocks, LANES), f32),
                pltpu.VMEM((windows, LANES), f32),
                pltpu.VMEM((windows, LANES), f32),
                pltpu.VMEM((groups, LANES), f32),
                *fall_here,
            ],
            compiler_params=grant,
            name="window_totals",
        )(exchange(own_den, "win"), near, used, far, fall)
        shared = exchange(own_total, "frame")
        if iteration < ITERS - 1:
            own_den = pl.pallas_call(
                next_kernel,
                out_shape=to_win,
                in_specs=[in_vmem] * 5 + [in_hbm],
                out_specs=in_vmem,
                scratch_shapes=den_scratch,
                compiler_params=grant,
                name="next_denominators",
            )(shared, counts, near, tops, far, fall)
    free_energy = pl.pallas_call(
        last_kernel,
        out_shape=jax.ShapeDtypeStruct((groups, LANES), f32),
        in_specs=[in_vmem],
        out_specs=in_vmem,
        compiler_params=grant,
        name="free_energies",
    )(shared)
    return free_energy.reshape(windows)


def solution(mesh):
    return jax.shard_map(
        on_device,
        mesh=mesh,
        in_specs=(P(None, "frame"), P("frame"), P(), P("win", None), P("win", None)),
        out_specs=P("win"),
        check_vma=False,
    )
```

```python
import functools
import math

import jax
import jax.numpy as jnp
from jax import lax
from jax.experimental import pallas as pl
from jax.experimental.pallas import tpu as pltpu
from jax.sharding import PartitionSpec as P


ITERS = 2
LANES = 128
ROWS = 64
STEP = 512

floor_value = -1e30
log2_e = 1.0 / math.log(2.0)
FAR = 384
FIRST = {"frame": 34, "win": 5}
least_sum = 2.0**-85
most_rate = 2.0**99

in_vmem = pl.BlockSpec(memory_space=pltpu.VMEM)
in_hbm = pl.BlockSpec(memory_space=pltpu.HBM)
grant = pltpu.CompilerParams(vmem_limit_bytes=12 << 20)


def hbm(array):
    return pltpu.with_memory_space_constraint(array, pltpu.HBM)


def log2(values):
    return jnp.log(values) * log2_e


def log2_sum(values):
    highest = jnp.max(values, axis=0)
    return highest + log2(jnp.sum(jnp.exp2(values - highest[None]), axis=0))


def together(pairs, sems):
    copies = [pltpu.make_async_copy(*pair, sems.at[place]) for place, pair in enumerate(pairs)]
    for copy in copies:
        copy.start()
    for copy in copies:
        copy.wait()


def count_kernel(lengths_hbm, ids_hbm, out_hbm, lengths_ref, ids_ref, out_ref, in_sems, out_sem):
    together([(lengths_hbm, lengths_ref), (ids_hbm, ids_ref)], in_sems)
    groups = out_ref.shape[1]
    capacity = ids_ref.shape[1]
    own_length = lengths_ref[lax.axis_index("frame")]
    local = ids_ref[...] - lax.axis_index("win") * (groups * LANES)
    slots = lax.broadcasted_iota(jnp.int32, (1, capacity), 1)
    local = jnp.where(slots < own_length, local, -1)
    group = jnp.where(local < 0, -1, lax.shift_right_logical(local, 7))
    place = jnp.bitwise_and(local, LANES - 1)
    in_group = lax.broadcasted_iota(jnp.int32, (8, capacity), 0) == group
    in_place = lax.broadcasted_iota(jnp.int32, (LANES, capacity), 0) == place
    counts = lax.dot_general(
        in_group.astype(jnp.float32).astype(jnp.bfloat16),
        in_place.astype(jnp.float32).astype(jnp.bfloat16),
        (((1,), (1,)), ((), ())),
        preferred_element_type=jnp.float32,
    )
    out_ref[...] = jnp.broadcast_to(counts[None, :groups], out_ref.shape)
    copy = pltpu.make_async_copy(out_ref, out_hbm, out_sem)
    copy.start()
    copy.wait()


def energy_kernel(
    stiffness_hbm, centers_hbm, distances_hbm, near_ref, tops_ref, far_hbm, fall_hbm,
    stiffness_ref, centers_ref, distances_ref, far_ref, fall_ref, in_sems, far_sem, fall_sems,
):
    together(
        [
            (stiffness_hbm, stiffness_ref),
            (centers_hbm, centers_ref),
            (distances_hbm, distances_ref),
        ],
        in_sems,
    )
    stiffness, centers = stiffness_ref[...] * log2_e, centers_ref[...]
    constant = jnp.sum(-0.5 * stiffness * centers * centers, axis=0, keepdims=True)
    first = lax.broadcasted_iota(jnp.int32, (8, constant.shape[1]), 0) == 0
    constant_rows = jnp.where(first, jnp.broadcast_to(constant, first.shape), 0.0)
    coef_rows = jnp.concatenate([stiffness * centers, -0.5 * stiffness, constant_rows], axis=0).T

    def send(index, start, size):
        columns = pl.ds(start, size)
        return pltpu.make_async_copy(fall_ref.at[:, columns], fall_hbm.at[:, columns], fall_sems.at[index])

    def one(index, start, size, to_ref, to):
        unit_rows = jnp.where(lax.broadcasted_iota(jnp.int32, (8, size), 0) == 0, 1.0, 0.0)
        separations = distances_ref[:, pl.ds(start, size)]
        features = jnp.concatenate([separations, separations * separations, unit_rows], axis=0)
        exponents = jnp.dot(
            coef_rows, features, precision=lax.Precision.HIGHEST, preferred_element_type=jnp.float32
        )
        top = jnp.max(exponents, axis=0, keepdims=True)
        fall = exponents - top
        fall_ref[:, pl.ds(start, size)] = fall
        send(index, start, size).start()
        to_ref[:, pl.ds(to, size)] = jnp.exp2(fall)
        for part in range(size // LANES):
            tops_ref[pl.ds(start // LANES + part, 1), :] = top[:, part * LANES : (part + 1) * LANES]

    near_frames, far_frames = near_ref.shape[1], far_ref.shape[1]
    copy = pltpu.make_async_copy(far_ref, far_hbm, far_sem)
    steps, rest = near_frames // STEP, near_frames % STEP
    one(steps, near_frames, far_frames, far_ref, 0)
    copy.start()

    def near(step, carry):
        start = pl.multiple_of(step * STEP, STEP)
        one(step, start, STEP, near_ref, start)
        return carry

    lax.fori_loop(0, steps, near, 0)
    if rest:
        one(steps + 1, near_frames - rest, rest, near_ref, near_frames - rest)
        send(steps + 1, near_frames - rest, rest).wait()
    copy.wait()
    send(steps, near_frames, far_frames).wait()
    for step in range(steps):
        send(step, step * STEP, STEP).wait()


def spread(row, to_ref):
    for group in range(row.shape[0]):
        lanes = jnp.broadcast_to(row[group : group + 1], (LANES, LANES))
        to_ref[group * LANES : (group + 1) * LANES, :] = lanes.T


def denominators(shifted, arrive, parts, fall_hbm, tops_ref, out_ref, scratch):
    column_ref, part_ref, row_ref, fall_ref, fall_sem = scratch
    most = jnp.max(jnp.max(shifted, axis=0, keepdims=True), axis=1, keepdims=True)
    spread(jnp.exp2(shifted - most), column_ref)
    windows = column_ref.shape[0]
    chunks = [slice(start, start + ROWS) for start in range(0, windows, ROWS)]

    def columns(block):
        return pl.ds(pl.multiple_of(block * LANES, LANES), LANES)

    def fold(values):
        return values.reshape(-1, 8, LANES)

    done = 0
    for part, ref in enumerate(parts):
        if part:
            arrive()
        count = ref.shape[1] // LANES

        def one(block, carry, ref=ref, done=done):
            sums = [jnp.sum(fold(ref[rows, columns(block)] * column_ref[rows, :]), axis=0) for rows in chunks]
            part_ref[done + block] = functools.reduce(jnp.add, sums)
            return carry

        lax.fori_loop(0, count, one, 0, unroll=True)
        done += count
    totals = jnp.sum(part_ref[...], axis=1)
    out_ref[...] = jnp.broadcast_to((tops_ref[...] + most + log2(totals))[None], out_ref.shape)

    @pl.when(jnp.min(totals) < least_sum)
    def _():
        copy = pltpu.make_async_copy(fall_hbm, fall_ref, fall_sem)
        copy.start()
        spread(shifted - most, column_ref)
        copy.wait()

        def exponents(rows, block):
            return fold(fall_ref[rows, columns(block)] + column_ref[rows, :])

        def exact(block, carry):
            tops = [jnp.max(exponents(rows, block), axis=0) for rows in chunks]
            highest = jnp.max(functools.reduce(jnp.maximum, tops), axis=0, keepdims=True)
            sums = [jnp.sum(jnp.exp2(exponents(rows, block) - highest), axis=0) for rows in chunks]
            total = jnp.sum(functools.reduce(jnp.add, sums), axis=0, keepdims=True)
            row_ref[pl.ds(block, 1), :] = highest + log2(total)
            return carry

        lax.fori_loop(0, row_ref.shape[0], exact, 0)
        out_ref[...] = jnp.broadcast_to((tops_ref[...] + most + row_ref[...])[None], out_ref.shape)


def first_kernel(
    lengths_hbm, shared_ref, near_ref, tops_ref, far_hbm, fall_hbm, counts_ref, out_ref, far_ref, used_ref,
    lengths_ref, sem, lengths_sem, *scratch,
):
    copy = pltpu.make_async_copy(far_hbm, far_ref, sem)
    lengths_copy = pltpu.make_async_copy(lengths_hbm, lengths_ref, lengths_sem)
    copy.start()
    lengths_copy.start()
    counts = jnp.sum(shared_ref[...], axis=0)
    counts_ref[...] = counts
    shifted = jnp.where(counts > 0.5, log2(jnp.maximum(counts, 1.0)), floor_value)
    denominators(shifted, copy.wait, (near_ref, far_ref), fall_hbm, tops_ref, out_ref, scratch)
    lengths_copy.wait()
    own_length = lengths_ref[lax.axis_index("frame")]
    slots = (
        lax.broadcasted_iota(jnp.int32, tops_ref.shape, 0) * LANES
        + lax.broadcasted_iota(jnp.int32, tops_ref.shape, 1)
    )
    used_ref[...] = jnp.where(slots < own_length, tops_ref[...], floor_value)


def next_kernel(shared_ref, counts_ref, near_ref, tops_ref, far_ref, fall_hbm, out_ref, *scratch):
    counts = counts_ref[...]
    free_energy = -log2_sum(shared_ref[...])
    shifted = jnp.where(counts > 0.5, log2(jnp.maximum(counts, 1.0)) + free_energy, floor_value)
    denominators(shifted, lambda: None, (near_ref, far_ref), fall_hbm, tops_ref, out_ref, scratch)


def window_kernel(
    shared_ref, near_ref, used_ref, far_ref, fall_hbm, out_ref, den_ref, rate_ref, top_ref, sum_ref, row_ref, fall_ref, fall_sem
):
    windows, blocks = near_ref.shape[0], den_ref.shape[0]
    groups = windows // LANES
    den = log2_sum(shared_ref[...]) - used_ref[...]
    den_ref[...] = den
    rates = jnp.exp2(-jnp.maximum(den, -100.0))
    rate_ref[...] = rates
    fastest = jnp.max(rates)

    def rows_of(chunk):
        return pl.ds(pl.multiple_of(chunk * ROWS, ROWS), ROWS)

    def one(chunk, carry):
        rows = rows_of(chunk)
        terms = (
            ref[rows, block * LANES : (block + 1) * LANES] * rate_ref[done + block : done + block + 1, :]
            for ref, done in ((near_ref, 0), (far_ref, near_ref.shape[1] // LANES))
            for block in range(ref.shape[1] // LANES)
        )
        sum_ref[rows, :] = functools.reduce(jnp.add, terms)
        return carry

    lax.fori_loop(0, windows // ROWS, one, 0)
    totals = []
    for group in range(groups):
        total = jnp.sum(sum_ref[group * LANES : (group + 1) * LANES, :].T, axis=0, keepdims=True)
        totals.append(total)
        row_ref[group : group + 1, :] = log2(total)
    out_ref[...] = jnp.broadcast_to(row_ref[...][None], out_ref.shape)
    lowest = jnp.min(functools.reduce(jnp.minimum, totals))
    in_range = jnp.logical_and(lowest > least_sum * jnp.maximum(fastest, 1.0), fastest < most_rate)

    @pl.when(jnp.logical_not(in_range))
    def _():
        copy = pltpu.make_async_copy(fall_hbm, fall_ref, fall_sem)
        copy.start()
        copy.wait()

        def exponents(rows, block):
            return fall_ref[rows, block * LANES : (block + 1) * LANES] - den_ref[block : block + 1, :]

        def exact(chunk, carry):
            rows = rows_of(chunk)
            top = functools.reduce(jnp.maximum, (exponents(rows, block) for block in range(blocks)))
            top_ref[rows, :] = top
            sum_ref[rows, :] = functools.reduce(
                jnp.add, (jnp.exp2(exponents(rows, block) - top) for block in range(blocks))
            )
            return carry

        lax.fori_loop(0, windows // ROWS, exact, 0)
        for group in range(groups):
            rows = slice(group * LANES, (group + 1) * LANES)
            tops, sums = top_ref[rows, :].T, sum_ref[rows, :].T
            top = jnp.max(tops, axis=0, keepdims=True)
            total = jnp.sum(sums * jnp.exp2(tops - top), axis=0, keepdims=True)
            row_ref[group : group + 1, :] = top + log2(total)
        out_ref[...] = jnp.broadcast_to(row_ref[...][None], out_ref.shape)


def last_kernel(shared_ref, out_ref):
    out_ref[...] = -math.log(2.0) * log2_sum(shared_ref[...])


def exchange(copies, axis):
    count = lax.axis_size(axis)
    order = [(member + FIRST[axis]) % count for member in range(count)]
    return lax.all_to_all(copies, axis, split_axis=0, concat_axis=0, tiled=True, axis_index_groups=[order])


def on_device(distances, sample_ids, lengths, stiffness, centers):
    windows, capacity = stiffness.shape[0], distances.shape[1]
    groups, blocks = windows // LANES, capacity // LANES
    f32, dma = jnp.float32, pltpu.SemaphoreType.DMA
    to_frame = jax.ShapeDtypeStruct((lax.axis_size("frame"), groups, LANES), f32)
    to_win = jax.ShapeDtypeStruct((lax.axis_size("win"), blocks, LANES), f32)
    lengths_here = pltpu.SMEM(lengths.shape, jnp.int32)
    local_counts = pl.pallas_call(
        count_kernel,
        out_shape=to_frame,
        in_specs=[in_hbm] * 2,
        out_specs=in_hbm,
        scratch_shapes=[
            lengths_here,
            pltpu.VMEM((1, capacity), jnp.int32),
            pltpu.VMEM(to_frame.shape, f32),
            dma((2,)),
            dma,
        ],
        name="count_windows",
    )(lengths, sample_ids.reshape(1, capacity))
    shared = exchange(local_counts, "frame")
    near_shape = jax.ShapeDtypeStruct((windows, capacity - FAR), f32)
    far_shape = jax.ShapeDtypeStruct((windows, FAR), f32)
    tops_shape = jax.ShapeDtypeStruct((blocks, LANES), f32)
    fall_here = [pltpu.VMEM((windows, capacity), f32), dma]
    near, tops, far, fall = pl.pallas_call(
        energy_kernel,
        out_shape=(
            near_shape,
            tops_shape,
            pltpu.HBM(far_shape.shape, f32),
            pltpu.HBM((windows, capacity), f32),
        ),
        in_specs=[in_hbm] * 3,
        out_specs=(in_vmem, in_vmem, in_hbm, in_hbm),
        scratch_shapes=[
            pltpu.VMEM((stiffness.shape[1], windows), f32),
            pltpu.VMEM((stiffness.shape[1], windows), f32),
            pltpu.VMEM(distances.shape, f32),
            pltpu.VMEM(far_shape.shape, f32),
            pltpu.VMEM((windows, capacity), f32),
            dma((3,)),
            dma,
            dma((capacity // STEP + 1,)),
        ],
        compiler_params=grant,
        cost_estimate=pl.CostEstimate(
            flops=24 * distances.shape[0] * windows * capacity,
            bytes_accessed=4 * windows * capacity,
            transcendentals=0,
        ),
        name="energies",
    )(hbm(stiffness.T), hbm(centers.T), hbm(distances))
    fall = hbm(fall)
    den_scratch = [
        pltpu.VMEM((windows, LANES), f32),
        pltpu.VMEM((blocks, 8, LANES), f32),
        pltpu.VMEM((blocks, LANES), f32),
        *fall_here,
    ]
    counts, own_den, far, used = pl.pallas_call(
        first_kernel,
        out_shape=(jax.ShapeDtypeStruct((groups, LANES), f32), to_win, far_shape, tops_shape),
        in_specs=[in_hbm, in_vmem, in_vmem, in_vmem, in_hbm, in_hbm],
        out_specs=(in_vmem,) * 4,
        scratch_shapes=[lengths_here, dma, dma, *den_scratch],
        compiler_params=grant,
        name="first_denominators",
    )(hbm(lengths), shared, near, tops, hbm(far), fall)
    for iteration in range(ITERS):
        own_total = pl.pallas_call(
            window_kernel,
            out_shape=to_frame,
            in_specs=[in_vmem] * 4 + [in_hbm],
            out_specs=in_vmem,
            scratch_shapes=[
                pltpu.VMEM((blocks, LANES), f32),
                pltpu.VMEM((blocks, LANES), f32),
                pltpu.VMEM((windows, LANES), f32),
                pltpu.VMEM((windows, LANES), f32),
                pltpu.VMEM((groups, LANES), f32),
                *fall_here,
            ],
            compiler_params=grant,
            name="window_totals",
        )(exchange(own_den, "win"), near, used, far, fall)
        shared = exchange(own_total, "frame")
        if iteration < ITERS - 1:
            own_den = pl.pallas_call(
                next_kernel,
                out_shape=to_win,
                in_specs=[in_vmem] * 5 + [in_hbm],
                out_specs=in_vmem,
                scratch_shapes=den_scratch,
                compiler_params=grant,
                name="next_denominators",
            )(shared, counts, near, tops, far, fall)
    free_energy = pl.pallas_call(
        last_kernel,
        out_shape=jax.ShapeDtypeStruct((groups, LANES), f32),
        in_specs=[in_vmem],
        out_specs=in_vmem,
        compiler_params=grant,
        name="free_energies",
    )(shared)
    return free_energy.reshape(windows)


def solution(mesh):
    return jax.shard_map(
        on_device,
        mesh=mesh,
        in_specs=(P(None, "frame"), P("frame"), P(), P("win", None), P("win", None)),
        out_specs=P("win"),
        check_vma=False,
    )
```
